32 devices in a mesh: dp: 4 (over y, core), pipe: 2 (over x), expert: 4 (over z).
Axes of the slice: x: 2, y: 2, z: 4, core: 2. Of those that a mesh axis runs over, the one named last changes fastest.
Arguments:
- activations: bfloat16 [2, 2048, 2048], P('pipe', ('dp', 'expert')), may hold values from -6 to 6
- out_grad: bfloat16 [2, 2048, 2048], P('pipe', ('dp', 'expert')), may hold values from -6 to 6
- slot_token: int32 [2, 16, 4, 4], P('pipe', ('dp', 'expert')), may hold values from 0 to 127, as said below
- slot_count: int32 [2, 16, 4], P('pipe', ('dp', 'expert')), may hold values from 0 to 4, as said below
- gate_prob: bfloat16 [2, 16, 4, 4], P('pipe', ('dp', 'expert')), may hold values from 0.049804688 to 1
- w_up: bfloat16 [2, 4, 2048, 768], P('pipe', 'expert'), may hold values from -0.125 to 0.125
- w_down: bfloat16 [2, 4, 768, 2048], P('pipe', 'expert'), may hold values from -0.21875 to 0.21875
Outputs:
- grad_prev: bfloat16 [2, 2048, 2048], P('pipe', ('dp', 'expert'))
- grad_gate: bfloat16 [2, 16, 4, 4], P('pipe', ('dp', 'expert'))
- grad_up: bfloat16 [2, 4, 2048, 768], P('pipe', 'expert', 'dp')
- grad_down: bfloat16 [2, 4, 768, 2048], P('pipe', 'expert', None, 'dp')
The draws below stay inside these ranges and needn't reach their ends.
Inputs may be any that keep to these rules, and one draw needn't show every extreme that they name: `slot_token`: the 4 slots of one source device and one expert name distinct tokens of that device. `slot_count`: in each section some expert gets 4 used slots from every source device; slots at or past the count are unused.
All inputs are finite; a program needn't handle non-finite values.
Results may differ from the reference program's by a relative error of at most 0.009.
Values may be sent and summed in bfloat16 or wider, within the bound.
No kernel may reach another device: no remote copies, remote signals or barrier semaphores. Data moves between devices by JAX's collectives and lax.ppermute only.
A program may use at most 64 MiB of HBM per device.

```python
import math
import jax
import jax.numpy as jnp
from jax import lax

D = 2048
FF = 768
TOK_DEV = 128
CAP = 4
SECTIONS = 2
GROUPS = 16
EXPERTS = 4
TOKENS = 2048
N_DP = 4
N_EXPERT = 4


def draw_slot_token(key, part):
    total_keys = SECTIONS * GROUPS * EXPERTS
    key_list = jax.random.split(key, total_keys)
    chosen = jax.vmap(lambda one_key: jax.random.permutation(one_key, TOK_DEV)[:CAP])(key_list)
    return chosen.reshape(SECTIONS, GROUPS, EXPERTS, CAP).astype(jnp.int32)


def draw_slot_count(key, part):
    key_pop, key_base, key_hot = jax.random.split(key, 3)
    popular = jax.random.randint(key_pop, (SECTIONS, 1, EXPERTS), 1, 3)
    base_counts = jax.random.randint(key_base, (SECTIONS, GROUPS, EXPERTS), 0, 2 * popular + 2)
    clipped = jnp.minimum(base_counts, CAP)
    hot_expert = jax.random.randint(key_hot, (SECTIONS, 1, 1), 0, EXPERTS)
    expert_ids = jnp.arange(EXPERTS)[None, None, :]
    return jnp.where(expert_ids == hot_expert, CAP, clipped).astype(jnp.int32)


def block_levels(rng, extent, cuts, smallest, top_value):
    factor_of = 1.0
    for dim, shards_of in cuts:
        draws = jax.random.uniform(jax.random.fold_in(jax.random.fold_in(rng, 6), dim), (shards_of,), jnp.float32, smallest / len(cuts), top_value / len(cuts))
        factor_of = factor_of * jnp.repeat(jnp.exp(draws), extent[dim] // shards_of).reshape((-1,) + (1,) * (len(extent) - 1 - dim))
    return factor_of


def scatter_about(key, shape, spread, limit, cuts=(), held_as=jnp.bfloat16):
    gain = block_levels(key, shape, cuts, -0.22, 0.18) if cuts else 1.0
    result = jax.random.normal(key, shape, jnp.float32) * spread * gain
    return jnp.minimum(jnp.maximum(result, -limit), limit).astype(held_as)


def setup_inputs(seed: int = 0) -> dict:
    keys = jax.random.split(jax.random.key(seed), 8)
    return {
        "activations": scatter_about(keys[0], (SECTIONS, TOKENS, D), 1.0, 6.0, ((0, 2), (1, 16))),
        "out_grad": scatter_about(keys[1], (SECTIONS, TOKENS, D), 1.0, 6.0, ((0, 2), (1, 16))),
        "slot_token": draw_slot_token(jax.random.fold_in(keys[7], 71), 0),
        "slot_count": draw_slot_count(jax.random.fold_in(keys[7], 71), 0),
        "gate_prob": jnp.clip(jnp.exp(math.log(1.0) - 2.9996462 * jax.random.uniform(keys[4], (SECTIONS, GROUPS, EXPERTS, CAP), jnp.float32) ** block_levels(keys[4], (SECTIONS, GROUPS, EXPERTS, CAP), ((0, 2), (1, 16)), -0.2, 0.2)), 0.049804688, 1.0).astype(jnp.bfloat16),
        "w_up": scatter_about(keys[5], (SECTIONS, EXPERTS, D, FF), D ** -0.5, 0.125, ((0, 2), (1, 4))),
        "w_down": scatter_about(keys[6], (SECTIONS, EXPERTS, FF, D), FF ** -0.5, 0.21875, ((0, 2), (1, 4))),
    }


def silu_slope(pre_values):
    logistic = jax.nn.sigmoid(pre_values)
    return logistic * (1.0 + pre_values * (1.0 - logistic))


def expert_pass(up_matrix, down_matrix, own_rows, own_grads, own_prob):
    pre_act = jnp.dot(own_rows, up_matrix, preferred_element_type=jnp.float32)
    hidden = jax.nn.silu(pre_act).astype(jnp.bfloat16)
    output_rows = jnp.dot(hidden, down_matrix, preferred_element_type=jnp.float32)
    gate_grad = jnp.sum(output_rows * own_grads.astype(jnp.float32), axis=-1).astype(jnp.bfloat16)
    scaled_grad = (own_prob.astype(jnp.float32)[:, None] * own_grads.astype(jnp.float32)).astype(jnp.bfloat16)
    hidden_grad = jnp.dot(scaled_grad, down_matrix.T, preferred_element_type=jnp.float32)
    act_grad = (hidden_grad * silu_slope(pre_act)).astype(jnp.bfloat16)
    row_grad = jnp.dot(act_grad, up_matrix.T, preferred_element_type=jnp.float32).astype(jnp.bfloat16)
    part_up = jnp.dot(own_rows.T, act_grad, preferred_element_type=jnp.float32).astype(jnp.bfloat16)
    part_down = jnp.dot(hidden.T, scaled_grad, preferred_element_type=jnp.float32).astype(jnp.bfloat16)
    return row_grad, gate_grad, part_up, part_down


def section_pass(up_section, down_section, section_acts, section_grads, slot_ids, counts, probs):
    groups = slot_ids.shape[0]
    token_rows = section_acts.reshape(groups, TOK_DEV, D)
    grad_rows = section_grads.reshape(groups, TOK_DEV, D)
    flat_ids = slot_ids.reshape(groups, EXPERTS * CAP).astype(jnp.int32)
    live_slot = jnp.arange(CAP)[None, None, :] < counts[:, :, None]
    pick_rows = jax.vmap(lambda source, positions: source[positions])
    sent_rows = pick_rows(token_rows, flat_ids).reshape(groups, EXPERTS, CAP, D)
    sent_grads = jnp.where(live_slot[..., None], pick_rows(grad_rows, flat_ids).reshape(groups, EXPERTS, CAP, D), 0).astype(jnp.bfloat16)
    sent_prob = jnp.where(live_slot, probs, 0).astype(jnp.bfloat16)

    def per_expert(items):
        up_matrix, down_matrix, rows_e, grads_e, prob_e = items
        rows_e = rows_e.reshape(N_DP, N_EXPERT * CAP, D)
        grads_e = grads_e.reshape(N_DP, N_EXPERT * CAP, D)
        prob_e = prob_e.reshape(N_DP, N_EXPERT * CAP)
        row_grad, gate_grad, part_up, part_down = jax.vmap(expert_pass, in_axes=(None, None, 0, 0, 0))(up_matrix, down_matrix, rows_e, grads_e, prob_e)
        part_up = lax.optimization_barrier(part_up)
        part_down = lax.optimization_barrier(part_down)
        summed_up = jnp.sum(part_up.astype(jnp.float32), axis=0).astype(jnp.bfloat16)
        summed_down = jnp.sum(part_down.astype(jnp.float32), axis=0).astype(jnp.bfloat16)
        return row_grad.reshape(groups, CAP, D), gate_grad.reshape(groups, CAP), summed_up, summed_down

    row_grads, gate_grads, summed_up, summed_down = lax.map(per_expert, (up_section, down_section, jnp.swapaxes(sent_rows, 0, 1), jnp.swapaxes(sent_grads, 0, 1), jnp.swapaxes(sent_prob, 0, 1)))
    row_grads = jnp.swapaxes(row_grads, 0, 1).reshape(groups, EXPERTS * CAP, D)
    gate_grads = jnp.swapaxes(gate_grads, 0, 1)
    one_hot = (flat_ids[:, :, None] == jnp.arange(TOK_DEV, dtype=jnp.int32)[None, None, :]).astype(jnp.float32)
    token_grad = jnp.einsum('gst,gsd->gtd', one_hot, row_grads.astype(jnp.float32)).astype(jnp.bfloat16)
    return token_grad.reshape(groups * TOK_DEV, D), gate_grads, summed_up, summed_down


def reference(activations, out_grad, slot_token, slot_count, gate_prob, w_up, w_down):
    token_list = []
    gate_list = []
    up_list = []
    down_list = []
    for section_index in range(SECTIONS):
        token_grad, gate_grads, summed_up, summed_down = section_pass(w_up[section_index], w_down[section_index], activations[section_index], out_grad[section_index], slot_token[section_index], slot_count[section_index], gate_prob[section_index])
        token_list.append(token_grad)
        gate_list.append(gate_grads)
        up_list.append(summed_up)
        down_list.append(summed_down)
    token_all = jnp.stack(token_list)
    grad_prev = jnp.concatenate([token_all[1:], jnp.zeros_like(token_all[:1])], axis=0)
    return grad_prev, jnp.stack(gate_list), jnp.stack(up_list), jnp.stack(down_list)
```

```python
import functools
import itertools

import jax
import jax.numpy as jnp
from jax import lax
from jax.experimental import pallas as pl
from jax.experimental.pallas import tpu as pltpu
from jax.sharding import PartitionSpec as P

BF16 = jnp.bfloat16
F32 = jnp.float32
LANES = 128
PERMUTE_LIMIT = 4


def row_marks(rows, width, capacity):
    row = lax.broadcasted_iota(jnp.int32, (rows, width), 0)
    inside = row & (2 * capacity - 1)
    group = lax.shift_right_logical(row, (2 * capacity).bit_length() - 1)
    return group, inside & (capacity - 1), inside < capacity


def stacked_rows(blocks, start, stop):
    return jnp.concatenate([block[:, start:stop].astype(F32) for block in blocks], axis=0)


def blocks_of(refs):
    if len(refs) == 1 and len(refs[0].shape) == 3:
        return [refs[0].at[k] for k in range(refs[0].shape[0])]
    return list(refs)


def own_place(axis, size):
    return lax.axis_index(axis) if size <= PERMUTE_LIMIT else 0


def pack_kernel(acts, grads, ids, counts, probs, *outs):
    tokens, width = acts.shape[1:]
    experts, capacity = ids.shape[2:]
    rows = 2 * experts * capacity
    place = own_place("expert", experts)
    group, slot, first = row_marks(rows, capacity, capacity)
    dest = group ^ place
    id_rows = ids[0, 0].astype(F32)
    prob_rows = probs[0, 0].astype(F32)
    id_grid = jnp.zeros((rows, capacity), F32)
    prob_grid = jnp.zeros((rows, capacity), F32)
    for e in range(experts):
        here = dest == e
        id_grid = jnp.where(here, id_rows[e : e + 1], id_grid)
        prob_grid = jnp.where(here, prob_rows[e : e + 1], prob_grid)
    at_slot = lax.broadcasted_iota(jnp.int32, (rows, capacity), 1) == slot
    id_col = jnp.sum(jnp.where(at_slot, id_grid, 0.0), axis=1, keepdims=True)
    prob_col = jnp.sum(jnp.where(at_slot, prob_grid, 0.0), axis=1, keepdims=True)
    dest_wide = row_marks(rows, experts, capacity)[0] ^ place
    at_dest = lax.broadcasted_iota(jnp.int32, (rows, experts), 1) == dest_wide
    count_row = counts[0].astype(F32)
    count_col = jnp.sum(jnp.where(at_dest, count_row, 0.0), axis=1, keepdims=True)
    live = slot[:, :1].astype(F32) < count_col
    prob_col = jnp.where(live, prob_col, 0.0)
    _, _, first_wide = row_marks(rows, tokens, capacity)
    lane = lax.broadcasted_iota(jnp.int32, (rows, tokens), 1).astype(F32)
    hit = jnp.where(lane == id_col, 1.0, 0.0)
    hit_live = jnp.where(live, hit, 0.0)
    pick_act = jnp.where(first_wide, hit, 0.0).astype(BF16)
    pick_grad = jnp.where(first_wide, 0.0, hit_live).astype(BF16)
    picked = jnp.dot(pick_act, acts[0], preferred_element_type=F32)
    picked = picked + jnp.dot(pick_grad, grads[0], preferred_element_type=F32)
    tail_lane = lax.broadcasted_iota(jnp.int32, (rows, LANES), 1)
    tail = jnp.where(tail_lane == 0, prob_col, jnp.where(tail_lane == 1, id_col, 0.0))
    size = 2 * capacity
    for k, out in enumerate(blocks_of(outs)):
        out[:, :width] = picked[k * size : (k + 1) * size].astype(BF16)
        out[:, width:] = tail[k * size : (k + 1) * size].astype(BF16)


def expert_kernel(capacity, replicas, n_blocks, *refs):
    blocks = blocks_of(refs[:n_blocks])
    up, down = refs[n_blocks : n_blocks + 2]
    outs = blocks_of(refs[n_blocks + 2 : -2])
    gate_out, scaled = refs[-2:]
    width, hidden_width = up.shape[2:]
    rows = 2 * capacity * len(blocks)
    part = width // replicas
    packed = stacked_rows(blocks, 0, width)
    tail = stacked_rows(blocks, width, width + LANES)
    prob = tail[:, 0:1]
    packed_bf16 = packed.astype(BF16)
    pre_act = jnp.dot(packed_bf16, up[0, 0], preferred_element_type=F32)
    grad_proj = lax.dot_general(
        packed_bf16, down[0, 0], (((1,), (1,)), ((), ())), preferred_element_type=F32
    )
    grad_proj = pltpu.roll(grad_proj, rows - capacity, 0)
    _, _, first_wide = row_marks(rows, width, capacity)
    scaled[...] = jnp.where(first_wide, packed, prob * packed).astype(BF16)
    logistic = jax.nn.sigmoid(pre_act)
    hidden = (pre_act * logistic).astype(BF16).astype(F32)
    slope = logistic * (1.0 + pre_act * (1.0 - logistic))
    act_grad = prob * grad_proj * slope
    gate = jnp.sum(hidden * grad_proj, axis=1, keepdims=True)
    lane = lax.broadcasted_iota(jnp.int32, (rows, LANES), 1)
    gate_out[...] = jnp.where(lane == 0, gate, tail).astype(BF16)
    _, _, first = row_marks(rows, hidden_width, capacity)
    both = jnp.where(first, act_grad, pltpu.roll(hidden, capacity, 0)).astype(BF16)
    place = own_place("dp", replicas)
    for k, out in enumerate(outs):
        column = pl.multiple_of((place ^ k) * part, LANES)
        out[:, :hidden_width] = both
        out[:, hidden_width:] = scaled[:, pl.ds(column, part)]


def back_kernel(capacity, own, up, gate_own, gate_other, *outs):
    width, hidden_width = up.shape[2:]
    rows = own.shape[0]
    half = width // 2
    row_grad = lax.dot_general(
        own[:, :hidden_width], up[0, 0], (((1,), (1,)), ((), ())), preferred_element_type=F32
    )
    _, _, first = row_marks(rows, half, capacity)
    body = jnp.where(first, row_grad[:, :half], pltpu.roll(row_grad[:, half:], capacity, 0))
    lane = lax.broadcasted_iota(jnp.int32, (rows, LANES), 1)
    tail = jnp.where(lane == 0, gate_other[...].astype(F32), gate_own[...].astype(F32))
    size = 2 * capacity
    for k, out in enumerate(blocks_of(outs)):
        out[:, :half] = body[k * size : (k + 1) * size].astype(BF16)
        out[:, half:] = tail[k * size : (k + 1) * size].astype(BF16)


def weight_kernel(capacity, n_blocks, *refs):
    blocks = blocks_of(refs[:n_blocks])
    grad_up, grad_down = refs[n_blocks:]
    hidden_width = grad_up.shape[3]
    joined = jnp.concatenate([block[...] for block in blocks], axis=0)
    both, sides = joined[:, :hidden_width], joined[:, hidden_width:]
    _, _, first = row_marks(both.shape[0], both.shape[1], capacity)
    act_grad = jnp.where(first, both, jnp.zeros_like(both))
    grad_up[0, 0] = lax.dot_general(
        sides, act_grad, (((0,), (0,)), ((), ())), preferred_element_type=F32
    ).astype(BF16)
    _, _, first = row_marks(sides.shape[0], sides.shape[1], capacity)
    scaled = jnp.where(first, jnp.zeros_like(sides), sides)
    grad_down[0, 0] = lax.dot_general(
        both, scaled, (((0,), (0,)), ((), ())), preferred_element_type=F32
    ).astype(BF16)


def combine_kernel(capacity, sections, n_blocks, *refs):
    blocks = blocks_of(refs[:n_blocks])
    grad_prev, grad_gate = refs[n_blocks:]
    tokens, width = grad_prev.shape[1:]
    experts = len(blocks)
    half = width // 2
    rows = 2 * capacity * experts
    body = stacked_rows(blocks, 0, half).astype(BF16)
    tail = stacked_rows(blocks, half, half + LANES)
    _, _, first = row_marks(rows, tokens, capacity)
    lane = lax.broadcasted_iota(jnp.int32, (rows, tokens), 1).astype(F32)
    kept = jnp.where(lax.axis_index("pipe") == sections - 1, 0.0, 1.0)
    hit = jnp.where(lane == tail[:, 1:2], kept, 0.0)
    for part, mark in enumerate((first, jnp.logical_not(first))):
        one_hot = jnp.where(mark, hit, 0.0).astype(BF16)
        grad_prev[0, :, part * half : (part + 1) * half] = lax.dot_general(
            one_hot, body, (((0,), (0,)), ((), ())), preferred_element_type=F32
        ).astype(BF16)
    _, slot, first = row_marks(rows, capacity, capacity)
    at_slot = lax.broadcasted_iota(jnp.int32, (rows, capacity), 1) == slot
    gates = jnp.where(jnp.logical_and(at_slot, first), tail[:, 0:1], 0.0).astype(BF16)
    column = lax.broadcasted_iota(jnp.int32, (experts, rows), 1)
    source = lax.shift_right_logical(column, (2 * capacity).bit_length() - 1)
    source = source ^ own_place("expert", experts)
    wanted = source == lax.broadcasted_iota(jnp.int32, (experts, rows), 0)
    grad_gate[0, 0] = jnp.dot(
        jnp.where(wanted, 1.0, 0.0).astype(BF16), gates, preferred_element_type=F32
    ).astype(BF16)


def call(kernel, name, out_shape, args, flops, n_bytes, scratch=()):
    whole = pl.BlockSpec(memory_space=pltpu.VMEM)
    return pl.pallas_call(
        kernel,
        name=name,
        out_shape=out_shape,
        in_specs=[whole] * len(args),
        out_specs=jax.tree.map(lambda _: whole, out_shape),
        scratch_shapes=list(scratch),
        cost_estimate=pl.CostEstimate(flops=flops, bytes_accessed=n_bytes, transcendentals=0),
    )(*args)


def permuted(block, axes, route):
    sizes = [lax.axis_size(axis) for axis in axes]

    def flat(place):
        return functools.reduce(lambda total, pair: total * pair[1] + pair[0], zip(place, sizes), 0)

    places = list(itertools.product(*[range(size) for size in sizes]))
    pairs = [(flat(place), flat(route(place))) for place in places]
    return lax.ppermute(block, axes if len(axes) > 1 else axes[0], pairs)


def message_shapes(count, rows, width):
    if count <= PERMUTE_LIMIT:
        return [jax.ShapeDtypeStruct((rows, width), BF16)] * count
    return [jax.ShapeDtypeStruct((count, rows, width), BF16)]


def exchanged(blocks, axis):
    if len(blocks) == 1:
        return [lax.all_to_all(blocks[0], axis, split_axis=0, concat_axis=0, tiled=True)]
    sent = [permuted(b, (axis,), lambda p, k=k: (p[0] ^ k,)) for k, b in enumerate(blocks) if k]
    return [blocks[0]] + sent


def sent_back(blocks, sections):
    if len(blocks) == 1:
        moved = permuted(blocks[0], ("pipe",), lambda p: ((p[0] - 1) % sections,))
        return [lax.all_to_all(moved, "expert", split_axis=0, concat_axis=0, tiled=True)]
    return [
        permuted(b, ("pipe", "expert"), lambda p, k=k: ((p[0] - 1) % sections, p[1] ^ k))
        for k, b in enumerate(blocks)
    ]


def per_device(activations, out_grad, slot_token, slot_count, gate_prob, w_up, w_down):
    tokens, width = activations.shape[1:]
    experts, capacity = slot_token.shape[2:]
    hidden_width = w_up.shape[3]
    replicas = lax.axis_size("dp")
    sections = lax.axis_size("pipe")
    size = 2 * capacity
    rows = size * experts
    part = width // replicas
    half = width // 2
    packed = call(
        pack_kernel,
        "pack",
        message_shapes(experts, size, width + LANES),
        (activations, out_grad, slot_token, slot_count, gate_prob),
        4 * rows * tokens * width,
        4 * tokens * width,
    )
    held = exchanged(packed, "expert")
    made = call(
        functools.partial(expert_kernel, capacity, replicas, len(held)),
        "expert",
        message_shapes(replicas, rows, hidden_width + part)
        + [jax.ShapeDtypeStruct((rows, LANES), BF16)],
        (*held, w_up, w_down),
        4 * rows * width * hidden_width,
        4 * width * hidden_width,
        [pltpu.VMEM((rows, width), BF16)],
    )
    shares, gate_own = made[:-1], made[-1]
    gate_other = permuted(gate_own, ("pipe",), lambda p: ((p[0] + 1) % sections,))
    joined = exchanged(shares, "dp")
    own = shares[0] if len(shares) > 1 else shares[0][0]
    back = call(
        functools.partial(back_kernel, capacity),
        "back",
        message_shapes(experts, size, half + LANES),
        (own, w_up, gate_own, gate_other),
        2 * rows * width * hidden_width,
        2 * width * hidden_width,
    )
    returned = sent_back(back, sections)
    grad_up, grad_down = call(
        functools.partial(weight_kernel, capacity, len(joined)),
        "weights",
        [
            jax.ShapeDtypeStruct((1, 1, part, hidden_width), BF16),
            jax.ShapeDtypeStruct((1, 1, hidden_width, part), BF16),
        ],
        tuple(joined),
        4 * replicas * rows * part * hidden_width,
        4 * part * hidden_width,
    )
    grad_prev, grad_gate = call(
        functools.partial(combine_kernel, capacity, sections, len(returned)),
        "combine",
        [
            jax.ShapeDtypeStruct((1, tokens, width), BF16),
            jax.ShapeDtypeStruct((1, 1, experts, capacity), BF16),
        ],
        tuple(returned),
        2 * rows * tokens * width,
        2 * tokens * width,
    )
    return grad_prev, grad_gate, grad_up, grad_down


def solution(mesh):
    by_token = ("dp", "expert")
    placed = (
        P("pipe", by_token, None),
        P("pipe", by_token, None),
        P("pipe", by_token, None, None),
        P("pipe", by_token, None),
        P("pipe", by_token, None, None),
        P("pipe", "expert", None, None),
        P("pipe", "expert", None, None),
    )
    return jax.shard_map(
        per_device,
        mesh=mesh,
        in_specs=placed,
        out_specs=(
            P("pipe", by_token, None),
            P("pipe", by_token, None, None),
            P("pipe", "expert", "dp", None),
            P("pipe", "expert", None, "dp"),
        ),
        check_vma=False,
    )
```

```python
import functools
import itertools

import jax
import jax.numpy as jnp
from jax import lax
from jax.experimental import pallas as pl
from jax.experimental.pallas import tpu as pltpu
from jax.sharding import PartitionSpec as P


BF16 = jnp.bfloat16
F32 = jnp.float32
LANES = 128
PERMUTE_LIMIT = 4
KERNEL_VMEM = 24 << 20


def row_marks(rows, width, capacity):
    row = lax.broadcasted_iota(jnp.int32, (rows, width), 0)
    inside = row & (2 * capacity - 1)
    group = lax.shift_right_logical(row, (2 * capacity).bit_length() - 1)
    return group, inside & (capacity - 1), inside < capacity


def stacked_rows(blocks, start, stop):
    return jnp.concatenate([block[:, start:stop].astype(F32) for block in blocks], axis=0)


def blocks_of(refs):
    if len(refs) == 1 and len(refs[0].shape) == 3:
        return [refs[0].at[k] for k in range(refs[0].shape[0])]
    return list(refs)


def own_place(axis, size):
    return lax.axis_index(axis) if size <= PERMUTE_LIMIT else 0


def pack_kernel(acts_far, grads_far, ids_far, counts_far, probs_far, *refs):
    outs, acts, grads, ids, counts, probs, sems = refs[:-6], *refs[-6:]
    near = (ids, counts, probs, acts, grads)
    far = (ids_far, counts_far, probs_far, acts_far, grads_far)
    copies = [pltpu.make_async_copy(a, b, sems.at[k]) for k, (a, b) in enumerate(zip(far, near))]
    for copy in copies:
        copy.start()
    for copy in copies[:3]:
        copy.wait()
    tokens, width = acts.shape[1:]
    experts, capacity = ids.shape[2:]
    rows = 2 * experts * capacity
    place = own_place("expert", experts)
    group, slot, _ = row_marks(rows, capacity, capacity)
    dest = group ^ place
    id_rows = ids[0, 0].astype(F32)
    prob_rows = probs[0, 0].astype(F32)
    id_grid = jnp.zeros((rows, capacity), F32)
    prob_grid = jnp.zeros((rows, capacity), F32)
    for e in range(experts):
        here = dest == e
        id_grid = jnp.where(here, id_rows[e : e + 1], id_grid)
        prob_grid = jnp.where(here, prob_rows[e : e + 1], prob_grid)
    at_slot = lax.broadcasted_iota(jnp.int32, (rows, capacity), 1) == slot
    id_col = jnp.sum(jnp.where(at_slot, id_grid, 0.0), axis=1, keepdims=True)
    prob_col = jnp.sum(jnp.where(at_slot, prob_grid, 0.0), axis=1, keepdims=True)
    dest_wide = row_marks(rows, experts, capacity)[0] ^ place
    at_dest = lax.broadcasted_iota(jnp.int32, (rows, experts), 1) == dest_wide
    count_row = counts[0].astype(F32)
    count_col = jnp.sum(jnp.where(at_dest, count_row, 0.0), axis=1, keepdims=True)
    live = slot[:, :1].astype(F32) < count_col
    prob_col = jnp.where(live, prob_col, 0.0)
    _, _, first_wide = row_marks(rows, tokens, capacity)
    lane = lax.broadcasted_iota(jnp.int32, (rows, tokens), 1).astype(F32)
    hit = jnp.where(lane == id_col, 1.0, 0.0)
    hit_live = jnp.where(live, hit, 0.0)
    pick_act = jnp.where(first_wide, hit, 0.0).astype(BF16)
    pick_grad = jnp.where(first_wide, 0.0, hit_live).astype(BF16)
    for copy in copies[3:]:
        copy.wait()
    picked = jnp.dot(pick_act, acts[0], preferred_element_type=F32)
    picked = picked + jnp.dot(pick_grad, grads[0], preferred_element_type=F32)
    tail_lane = lax.broadcasted_iota(jnp.int32, (rows, LANES), 1)
    tail = jnp.where(tail_lane == 0, prob_col, jnp.where(tail_lane == 1, id_col, 0.0))
    size = 2 * capacity
    for k, out in enumerate(blocks_of(outs)):
        out[:, :width] = picked[k * size : (k + 1) * size].astype(BF16)
        out[:, width:] = tail[k * size : (k + 1) * size].astype(BF16)


def load_kernel(up_far, down_far, _, up, down, sems):
    copies = [
        pltpu.make_async_copy(up_far, up, sems.at[0]),
        pltpu.make_async_copy(down_far, down, sems.at[1]),
    ]
    for copy in copies:
        copy.start()
    for copy in copies:
        copy.wait()


def expert_kernel(capacity, replicas, n_blocks, *refs):
    blocks = blocks_of(refs[:n_blocks])
    up, down = refs[n_blocks : n_blocks + 2]
    outs = blocks_of(refs[n_blocks + 2 : -2])
    gate_out, scaled = refs[-2:]
    width, hidden_width = up.shape[2:]
    rows = 2 * capacity * len(blocks)
    part = width // replicas
    packed = stacked_rows(blocks, 0, width)
    tail = stacked_rows(blocks, width, width + LANES)
    prob = tail[:, 0:1]
    packed_bf16 = packed.astype(BF16)
    pre_act = jnp.dot(packed_bf16, up[0, 0], preferred_element_type=F32)
    grad_proj = lax.dot_general(
        packed_bf16, down[0, 0], (((1,), (1,)), ((), ())), preferred_element_type=F32
    )
    grad_proj = pltpu.roll(grad_proj, rows - capacity, 0)
    _, _, first_wide = row_marks(rows, width, capacity)
    scaled[...] = jnp.where(first_wide, packed, prob * packed).astype(BF16)
    logistic = jax.nn.sigmoid(pre_act)
    hidden = (pre_act * logistic).astype(BF16).astype(F32)
    slope = logistic * (1.0 + pre_act * (1.0 - logistic))
    act_grad = prob * grad_proj * slope
    gate = jnp.sum(hidden * grad_proj, axis=1, keepdims=True)
    lane = lax.broadcasted_iota(jnp.int32, (rows, LANES), 1)
    gate_out[...] = jnp.where(lane == 0, gate, tail).astype(BF16)
    _, _, first = row_marks(rows, hidden_width, capacity)
    both = jnp.where(first, act_grad, pltpu.roll(hidden, capacity, 0)).astype(BF16)
    place = own_place("dp", replicas)
    for k, out in enumerate(outs):
        column = pl.multiple_of((place ^ k) * part, LANES)
        out[:, :hidden_width] = both
        out[:, hidden_width:] = scaled[:, pl.ds(column, part)]


def back_kernel(capacity, own, up, gate_own, gate_other, *outs):
    width, hidden_width = up.shape[2:]
    rows = own.shape[0]
    half = width // 2
    row_grad = lax.dot_general(
        own[:, :hidden_width], up[0, 0], (((1,), (1,)), ((), ())), preferred_element_type=F32
    )
    _, _, first = row_marks(rows, half, capacity)
    body = jnp.where(first, row_grad[:, :half], pltpu.roll(row_grad[:, half:], capacity, 0))
    lane = lax.broadcasted_iota(jnp.int32, (rows, LANES), 1)
    tail = jnp.where(lane == 0, gate_other[...].astype(F32), gate_own[...].astype(F32))
    size = 2 * capacity
    for k, out in enumerate(blocks_of(outs)):
        out[:, :half] = body[k * size : (k + 1) * size].astype(BF16)
        out[:, half:] = tail[k * size : (k + 1) * size].astype(BF16)


def weight_kernel(capacity, n_blocks, *refs):
    blocks = blocks_of(refs[:n_blocks])
    grad_up, grad_down = refs[n_blocks:]
    hidden_width = grad_up.shape[3]
    joined = jnp.concatenate([block[...] for block in blocks], axis=0)
    both, sides = joined[:, :hidden_width], joined[:, hidden_width:]
    _, _, first = row_marks(both.shape[0], both.shape[1], capacity)
    act_grad = jnp.where(first, both, jnp.zeros_like(both))
    grad_up[0, 0] = lax.dot_general(
        sides, act_grad, (((0,), (0,)), ((), ())), preferred_element_type=F32
    ).astype(BF16)
    _, _, first = row_marks(sides.shape[0], sides.shape[1], capacity)
    scaled = jnp.where(first, jnp.zeros_like(sides), sides)
    grad_down[0, 0] = lax.dot_general(
        both, scaled, (((0,), (0,)), ((), ())), preferred_element_type=F32
    ).astype(BF16)


def combine_kernel(capacity, sections, n_blocks, *refs):
    blocks = blocks_of(refs[:n_blocks])
    grad_prev, grad_gate = refs[n_blocks:]
    tokens, width = grad_prev.shape[1:]
    experts = len(blocks)
    half = width // 2
    rows = 2 * capacity * experts
    body = stacked_rows(blocks, 0, half).astype(BF16)
    tail = stacked_rows(blocks, half, half + LANES)
    _, _, first = row_marks(rows, tokens, capacity)
    lane = lax.broadcasted_iota(jnp.int32, (rows, tokens), 1).astype(F32)
    kept = jnp.where(lax.axis_index("pipe") == sections - 1, 0.0, 1.0)
    hit = jnp.where(lane == tail[:, 1:2], kept, 0.0)
    for part, mark in enumerate((first, jnp.logical_not(first))):
        one_hot = jnp.where(mark, hit, 0.0).astype(BF16)
        grad_prev[0, :, part * half : (part + 1) * half] = lax.dot_general(
            one_hot, body, (((0,), (0,)), ((), ())), preferred_element_type=F32
        ).astype(BF16)
    _, slot, first = row_marks(rows, capacity, capacity)
    at_slot = lax.broadcasted_iota(jnp.int32, (rows, capacity), 1) == slot
    gates = jnp.where(jnp.logical_and(at_slot, first), tail[:, 0:1], 0.0).astype(BF16)
    column = lax.broadcasted_iota(jnp.int32, (experts, rows), 1)
    source = lax.shift_right_logical(column, (2 * capacity).bit_length() - 1)
    source = source ^ own_place("expert", experts)
    wanted = source == lax.broadcasted_iota(jnp.int32, (experts, rows), 0)
    grad_gate[0, 0] = jnp.dot(
        jnp.where(wanted, 1.0, 0.0).astype(BF16), gates, preferred_element_type=F32
    ).astype(BF16)


def call(kernel, out_shape, args, flops, n_bytes, scratch=(), far=(), near_out=True):
    near_spec = pl.BlockSpec(memory_space=pltpu.VMEM)
    far_spec = pl.BlockSpec(memory_space=pl.ANY)
    args = [
        pltpu.with_memory_space_constraint(a, pltpu.HBM if k in far else pltpu.VMEM)
        for k, a in enumerate(args)
    ]
    if near_out:
        out_shape = [pltpu.VMEM(s.shape, s.dtype) for s in out_shape]
    return pl.pallas_call(
        kernel,
        out_shape=out_shape,
        in_specs=[far_spec if k in far else near_spec for k in range(len(args))],
        out_specs=[near_spec] * len(out_shape),
        scratch_shapes=list(scratch),
        compiler_params=pltpu.CompilerParams(vmem_limit_bytes=KERNEL_VMEM),
        cost_estimate=pl.CostEstimate(flops=flops, bytes_accessed=n_bytes, transcendentals=0),
    )(*args)


def permuted(block, axes, route):
    sizes = [lax.axis_size(axis) for axis in axes]

    def flat(place):
        return functools.reduce(lambda total, pair: total * pair[1] + pair[0], zip(place, sizes), 0)

    places = list(itertools.product(*[range(size) for size in sizes]))
    pairs = [(flat(place), flat(route(place))) for place in places]
    return lax.ppermute(block, axes if len(axes) > 1 else axes[0], pairs)


def message_shapes(count, rows, width):
    if count <= PERMUTE_LIMIT:
        return [jax.ShapeDtypeStruct((rows, width), BF16)] * count
    return [jax.ShapeDtypeStruct((count, rows, width), BF16)]


def exchanged(blocks, axis):
    if len(blocks) == 1:
        return [lax.all_to_all(blocks[0], axis, split_axis=0, concat_axis=0, tiled=True)]
    sent = [
        permuted(b, (axis,), lambda p, k=k: (p[0] ^ k,))
        for k, b in enumerate(blocks)
        if k
    ]
    return [blocks[0]] + sent


def sent_back(blocks, sections):
    if len(blocks) == 1:
        moved = permuted(blocks[0], ("pipe",), lambda p: ((p[0] - 1) % sections,))
        return [lax.all_to_all(moved, "expert", split_axis=0, concat_axis=0, tiled=True)]
    return [
        permuted(b, ("pipe", "expert"), lambda p, k=k: ((p[0] - 1) % sections, p[1] ^ k))
        for k, b in enumerate(blocks)
    ]


def per_device(activations, out_grad, slot_token, slot_count, gate_prob, w_up, w_down):
    tokens, width = activations.shape[1:]
    experts, capacity = slot_token.shape[2:]
    hidden_width = w_up.shape[3]
    replicas = lax.axis_size("dp")
    sections = lax.axis_size("pipe")
    size = 2 * capacity
    rows = size * experts
    part = width // replicas
    half = width // 2
    sources = (activations, out_grad, slot_token, slot_count, gate_prob)
    packed = call(
        pack_kernel,
        message_shapes(experts, size, width + LANES),
        sources,
        4 * rows * tokens * width,
        4 * tokens * width,
        [pltpu.VMEM(a.shape, a.dtype) for a in sources] + [pltpu.SemaphoreType.DMA((5,))],
        far=range(5),
    )
    near_up, near_down = call(
        load_kernel,
        [jax.ShapeDtypeStruct(w.shape, w.dtype) for w in (w_up, w_down)],
        (w_up, w_down, packed[0]),
        0,
        4 * width * hidden_width,
        [pltpu.SemaphoreType.DMA((2,))],
        far=range(2),
    )
    held = exchanged(packed, "expert")
    made = call(
        functools.partial(expert_kernel, capacity, replicas, len(held)),
        message_shapes(replicas, rows, hidden_width + part)
        + [jax.ShapeDtypeStruct((rows, LANES), BF16)],
        (*held, near_up, near_down),
        4 * rows * width * hidden_width,
        4 * width * hidden_width,
        [pltpu.VMEM((rows, width), BF16)],
    )
    shares, gate_own = made[:-1], made[-1]
    gate_other = permuted(gate_own, ("pipe",), lambda p: ((p[0] + 1) % sections,))
    joined = exchanged(shares, "dp")
    own = shares[0] if len(shares) > 1 else shares[0][0]
    back = call(
        functools.partial(back_kernel, capacity),
        message_shapes(experts, size, half + LANES),
        (own, near_up, gate_own, gate_other),
        2 * rows * width * hidden_width,
        2 * width * hidden_width,
    )
    returned = sent_back(back, sections)
    grad_up, grad_down = call(
        functools.partial(weight_kernel, capacity, len(joined)),
        [
            jax.ShapeDtypeStruct((1, 1, part, hidden_width), BF16),
            jax.ShapeDtypeStruct((1, 1, hidden_width, part), BF16),
        ],
        tuple(joined),
        4 * replicas * rows * part * hidden_width,
        4 * part * hidden_width,
        near_out=False,
    )
    grad_prev, grad_gate = call(
        functools.partial(combine_kernel, capacity, sections, len(returned)),
        [
            jax.ShapeDtypeStruct((1, tokens, width), BF16),
            jax.ShapeDtypeStruct((1, 1, experts, capacity), BF16),
        ],
        tuple(returned),
        2 * rows * tokens * width,
        2 * tokens * width,
        near_out=False,
    )
    return grad_prev, grad_gate, grad_up, grad_down


def solution(mesh):
    by_token = ("dp", "expert")
    placed = (
        P("pipe", by_token, None),
        P("pipe", by_token, None),
        P("pipe", by_token, None, None),
        P("pipe", by_token, None),
        P("pipe", by_token, None, None),
        P("pipe", "expert", None, None),
        P("pipe", "expert", None, None),
    )
    return jax.shard_map(
        per_device,
        mesh=mesh,
        in_specs=placed,
        out_specs=(
            P("pipe", by_token, None),
            P("pipe", by_token, None, None),
            P("pipe", "expert", "dp", None),
            P("pipe", "expert", None, "dp"),
        ),
        check_vma=False,
    )
```

```python
import functools
import itertools

import jax
import jax.numpy as jnp
from jax import lax
from jax.experimental import pallas as pl
from jax.experimental.pallas import tpu as pltpu
from jax.sharding import PartitionSpec as P


BF16 = jnp.bfloat16
F32 = jnp.float32
LANES = 128
PERMUTE_LIMIT = 4
KERNEL_VMEM = 24 << 20


def row_marks(rows, width, capacity):
    row = lax.broadcasted_iota(jnp.int32, (rows, width), 0)
    inside = row & (2 * capacity - 1)
    group = lax.shift_right_logical(row, (2 * capacity).bit_length() - 1)
    return group, inside & (capacity - 1), inside < capacity


def stacked_rows(blocks, start, stop):
    return jnp.concatenate([block[:, start:stop].astype(F32) for block in blocks], axis=0)


def blocks_of(refs):
    if len(refs) == 1 and len(refs[0].shape) == 3:
        return [refs[0].at[k] for k in range(refs[0].shape[0])]
    return list(refs)


def own_place(axis, size):
    return lax.axis_index(axis) if size <= PERMUTE_LIMIT else 0


def pack_kernel(acts_far, grads_far, ids_far, counts_far, probs_far, *refs):
    outs, acts, grads, ids, counts, probs, sems = refs[:-6], *refs[-6:]
    near = (ids, counts, probs, acts, grads)
    far = (ids_far, counts_far, probs_far, acts_far, grads_far)
    copies = [pltpu.make_async_copy(a, b, sems.at[k]) for k, (a, b) in enumerate(zip(far, near))]
    for copy in copies:
        copy.start()
    for copy in copies[:3]:
        copy.wait()
    tokens, width = acts.shape[1:]
    experts, capacity = ids.shape[2:]
    rows = 2 * experts * capacity
    place = own_place("expert", experts)
    group, slot, _ = row_marks(rows, capacity, capacity)
    dest = group ^ place
    id_rows = ids[0, 0].astype(F32)
    prob_rows = probs[0, 0].astype(F32)
    id_grid = jnp.zeros((rows, capacity), F32)
    prob_grid = jnp.zeros((rows, capacity), F32)
    for e in range(experts):
        here = dest == e
        id_grid = jnp.where(here, id_rows[e : e + 1], id_grid)
        prob_grid = jnp.where(here, prob_rows[e : e + 1], prob_grid)
    at_slot = lax.broadcasted_iota(jnp.int32, (rows, capacity), 1) == slot
    id_col = jnp.sum(jnp.where(at_slot, id_grid, 0.0), axis=1, keepdims=True)
    prob_col = jnp.sum(jnp.where(at_slot, prob_grid, 0.0), axis=1, keepdims=True)
    dest_wide = row_marks(rows, experts, capacity)[0] ^ place
    at_dest = lax.broadcasted_iota(jnp.int32, (rows, experts), 1) == dest_wide
    count_row = counts[0].astype(F32)
    count_col = jnp.sum(jnp.where(at_dest, count_row, 0.0), axis=1, keepdims=True)
    live = slot[:, :1].astype(F32) < count_col
    prob_col = jnp.where(live, prob_col, 0.0)
    _, _, first_wide = row_marks(rows, tokens, capacity)
    lane = lax.broadcasted_iota(jnp.int32, (rows, tokens), 1).astype(F32)
    hit = jnp.where(lane == id_col, 1.0, 0.0)
    hit_live = jnp.where(live, hit, 0.0)
    pick_act = jnp.where(first_wide, hit, 0.0).astype(BF16)
    pick_grad = jnp.where(first_wide, 0.0, hit_live).astype(BF16)
    for copy in copies[3:]:
        copy.wait()
    picked = jnp.dot(pick_act, acts[0], preferred_element_type=F32)
    picked = picked + jnp.dot(pick_grad, grads[0], preferred_element_type=F32)
    tail_lane = lax.broadcasted_iota(jnp.int32, (rows, LANES), 1)
    tail = jnp.where(tail_lane == 0, prob_col, jnp.where(tail_lane == 1, id_col, 0.0))
    size = 2 * capacity
    for k, out in enumerate(blocks_of(outs)):
        out[:, :width] = picked[k * size : (k + 1) * size].astype(BF16)
        out[:, width:] = tail[k * size : (k + 1) * size].astype(BF16)


def load_kernel(up_far, down_far, _, up, down, sems):
    copies = [
        pltpu.make_async_copy(up_far, up, sems.at[0]),
        pltpu.make_async_copy(down_far, down, sems.at[1]),
    ]
    for copy in copies:
        copy.start()
    for copy in copies:
        copy.wait()


def expert_kernel(capacity, replicas, n_blocks, *refs):
    blocks = blocks_of(refs[:n_blocks])
    up, down = refs[n_blocks : n_blocks + 2]
    outs = blocks_of(refs[n_blocks + 2 : -2])
    tail_out, scaled = refs[-2:]
    width, hidden_width = up.shape[2:]
    rows = 2 * capacity * len(blocks)
    part = width // replicas
    packed = stacked_rows(blocks, 0, width)
    tail = stacked_rows(blocks, width, width + LANES)
    prob = tail[:, 0:1]
    packed_bf16 = packed.astype(BF16)
    pre_act = jnp.dot(packed_bf16, up[0, 0], preferred_element_type=F32)
    grad_proj = lax.dot_general(
        packed_bf16, down[0, 0], (((1,), (1,)), ((), ())), preferred_element_type=F32
    )
    grad_proj = pltpu.roll(grad_proj, rows - capacity, 0)
    _, _, first_wide = row_marks(rows, width, capacity)
    scaled[...] = jnp.where(first_wide, packed, prob * packed).astype(BF16)
    logistic = jax.nn.sigmoid(pre_act)
    hidden = (pre_act * logistic).astype(BF16).astype(F32)
    slope = logistic * (1.0 + pre_act * (1.0 - logistic))
    act_grad = prob * grad_proj * slope
    gate = jnp.sum(hidden * grad_proj, axis=1, keepdims=True)
    lane = lax.broadcasted_iota(jnp.int32, (rows, LANES), 1)
    tail_out[...] = jnp.where(lane == 0, gate, tail).astype(BF16)
    _, _, first = row_marks(rows, hidden_width, capacity)
    both = jnp.where(first, act_grad, pltpu.roll(hidden, capacity, 0)).astype(BF16)
    place = own_place("dp", replicas)
    for k, out in enumerate(outs):
        wide = out.shape[1] - hidden_width
        column = pl.multiple_of((place ^ k) // (wide // part) * wide, LANES)
        out[:, :hidden_width] = both
        out[:, hidden_width:] = scaled[:, pl.ds(column, wide)]


def back_kernel(capacity, own, up, tail, out):
    width, hidden_width = up.shape[2:]
    half = width // 2
    row_grad = lax.dot_general(
        own[:, :hidden_width], up[0, 0], (((1,), (1,)), ((), ())), preferred_element_type=F32
    )
    _, _, first = row_marks(own.shape[0], half, capacity)
    upper = pltpu.roll(row_grad[:, half:], capacity, 0)
    out[:, :half] = jnp.where(first, row_grad[:, :half], upper).astype(BF16)
    out[:, half:] = tail[...]


def reply_kernel(capacity, body, tail_own, *outs):
    half = body.shape[1] - LANES
    rows = body.shape[0]
    lane = lax.broadcasted_iota(jnp.int32, (rows, LANES), 1)
    tail = jnp.where(lane == 0, tail_own[...].astype(F32), body[:, half:].astype(F32))
    size = 2 * capacity
    for k, out in enumerate(blocks_of(outs)):
        out[:, :half] = body[k * size : (k + 1) * size, :half]
        out[:, half:] = tail[k * size : (k + 1) * size].astype(BF16)


def weight_kernel(capacity, n_blocks, *refs):
    blocks = blocks_of(refs[:n_blocks])
    grad_up, grad_down = refs[n_blocks:]
    hidden_width = grad_up.shape[3]
    part = grad_up.shape[2]
    both = jnp.concatenate([block[:, :hidden_width] for block in blocks], axis=0)
    columns = []
    for block in blocks:
        if block.shape[1] > hidden_width + part:
            begin = hidden_width + (lax.axis_index("dp") & 1) * part
            columns.append(block[:, pl.ds(pl.multiple_of(begin, LANES), part)])
        else:
            columns.append(block[:, hidden_width:])
    sides = jnp.concatenate(columns, axis=0)
    _, _, first = row_marks(both.shape[0], both.shape[1], capacity)
    act_grad = jnp.where(first, both, jnp.zeros_like(both))
    grad_up[0, 0] = lax.dot_general(
        sides, act_grad, (((0,), (0,)), ((), ())), preferred_element_type=F32
    ).astype(BF16)
    _, _, first = row_marks(sides.shape[0], sides.shape[1], capacity)
    scaled = jnp.where(first, jnp.zeros_like(sides), sides)
    grad_down[0, 0] = lax.dot_general(
        both, scaled, (((0,), (0,)), ((), ())), preferred_element_type=F32
    ).astype(BF16)


def combine_kernel(capacity, sections, n_blocks, *refs):
    blocks = blocks_of(refs[:n_blocks])
    grad_prev, grad_gate = refs[n_blocks:]
    tokens, width = grad_prev.shape[1:]
    experts = len(blocks)
    half = width // 2
    rows = 2 * capacity * experts
    body = stacked_rows(blocks, 0, half).astype(BF16)
    tail = stacked_rows(blocks, half, half + LANES)
    _, _, first = row_marks(rows, tokens, capacity)
    lane = lax.broadcasted_iota(jnp.int32, (rows, tokens), 1).astype(F32)
    kept = jnp.where(lax.axis_index("pipe") == sections - 1, 0.0, 1.0)
    hit = jnp.where(lane == tail[:, 1:2], kept, 0.0)
    for part, mark in enumerate((first, jnp.logical_not(first))):
        one_hot = jnp.where(mark, hit, 0.0).astype(BF16)
        grad_prev[0, :, part * half : (part + 1) * half] = lax.dot_general(
            one_hot, body, (((0,), (0,)), ((), ())), preferred_element_type=F32
        ).astype(BF16)
    _, slot, first = row_marks(rows, capacity, capacity)
    at_slot = lax.broadcasted_iota(jnp.int32, (rows, capacity), 1) == slot
    gates = jnp.where(jnp.logical_and(at_slot, first), tail[:, 0:1], 0.0).astype(BF16)
    column = lax.broadcasted_iota(jnp.int32, (experts, rows), 1)
    source = lax.shift_right_logical(column, (2 * capacity).bit_length() - 1)
    source = source ^ own_place("expert", experts)
    wanted = source == lax.broadcasted_iota(jnp.int32, (experts, rows), 0)
    grad_gate[0, 0] = jnp.dot(
        jnp.where(wanted, 1.0, 0.0).astype(BF16), gates, preferred_element_type=F32
    ).astype(BF16)


def call(kernel, out_shape, args, flops, n_bytes, scratch=(), far=(), near_out=True):
    near_spec = pl.BlockSpec(memory_space=pltpu.VMEM)
    far_spec = pl.BlockSpec(memory_space=pl.ANY)
    args = [
        pltpu.with_memory_space_constraint(a, pltpu.HBM if k in far else pltpu.VMEM)
        for k, a in enumerate(args)
    ]
    if near_out:
        out_shape = [pltpu.VMEM(s.shape, s.dtype) for s in out_shape]
    return pl.pallas_call(
        kernel,
        out_shape=out_shape,
        in_specs=[far_spec if k in far else near_spec for k in range(len(args))],
        out_specs=[near_spec] * len(out_shape),
        scratch_shapes=list(scratch),
        compiler_params=pltpu.CompilerParams(vmem_limit_bytes=KERNEL_VMEM),
        cost_estimate=pl.CostEstimate(flops=flops, bytes_accessed=n_bytes, transcendentals=0),
    )(*args)


def permuted(block, axes, route):
    sizes = [lax.axis_size(axis) for axis in axes]

    def flat(place):
        return functools.reduce(lambda total, pair: total * pair[1] + pair[0], zip(place, sizes), 0)

    places = list(itertools.product(*[range(size) for size in sizes]))
    pairs = [(flat(place), flat(route(place))) for place in places]
    return lax.ppermute(block, axes if len(axes) > 1 else axes[0], pairs)


def message_shapes(count, rows, width):
    if count <= PERMUTE_LIMIT:
        return [jax.ShapeDtypeStruct((rows, width), BF16)] * count
    return [jax.ShapeDtypeStruct((count, rows, width), BF16)]


def exchanged(blocks, axis):
    if len(blocks) == 1:
        return [lax.all_to_all(blocks[0], axis, split_axis=0, concat_axis=0, tiled=True)]
    sent = [
        permuted(b, (axis,), lambda p, k=k: (p[0] ^ k,))
        for k, b in enumerate(blocks)
        if k
    ]
    return [blocks[0]] + sent


def share_shapes(replicas, rows, hidden_width, part):
    if replicas != 4:
        return message_shapes(replicas, rows, hidden_width + part)
    widths = (hidden_width + part, hidden_width + part, hidden_width + 2 * part)
    return [jax.ShapeDtypeStruct((rows, width), BF16) for width in widths]


def shared(blocks, replicas):
    if replicas != 4:
        return exchanged(blocks, "dp")
    own, near, far = blocks
    crossed = permuted(far, ("dp",), lambda p: (p[0] ^ 2,))
    beside = permuted(near, ("dp",), lambda p: (p[0] ^ 1,))
    passed = permuted(crossed, ("dp",), lambda p: (p[0] ^ 1,))
    return [own, beside, crossed, passed]


def per_device(activations, out_grad, slot_token, slot_count, gate_prob, w_up, w_down):
    tokens, width = activations.shape[1:]
    experts, capacity = slot_token.shape[2:]
    hidden_width = w_up.shape[3]
    replicas = lax.axis_size("dp")
    sections = lax.axis_size("pipe")
    size = 2 * capacity
    rows = size * experts
    part = width // replicas
    half = width // 2
    sources = (activations, out_grad, slot_token, slot_count, gate_prob)
    packed = call(
        pack_kernel,
        message_shapes(experts, size, width + LANES),
        sources,
        4 * rows * tokens * width,
        4 * tokens * width,
        [pltpu.VMEM(a.shape, a.dtype) for a in sources] + [pltpu.SemaphoreType.DMA((5,))],
        far=range(5),
    )
    near_up, near_down = call(
        load_kernel,
        [jax.ShapeDtypeStruct(w.shape, w.dtype) for w in (w_up, w_down)],
        (w_up, w_down, packed[0]),
        0,
        4 * width * hidden_width,
        [pltpu.SemaphoreType.DMA((2,))],
        far=range(2),
    )
    held = exchanged(packed, "expert")
    made = call(
        functools.partial(expert_kernel, capacity, replicas, len(held)),
        share_shapes(replicas, rows, hidden_width, part)
        + [jax.ShapeDtypeStruct((rows, LANES), BF16)],
        (*held, near_up, near_down),
        4 * rows * width * hidden_width,
        4 * width * hidden_width,
        [pltpu.VMEM((rows, width), BF16)],
    )
    shares, tail_own = made[:-1], made[-1]
    joined = shared(shares, replicas)
    own = shares[0] if len(shares) > 1 else shares[0][0]
    (body,) = call(
        functools.partial(back_kernel, capacity),
        [jax.ShapeDtypeStruct((rows, half + LANES), BF16)],
        (own, near_up, tail_own),
        2 * rows * width * hidden_width,
        2 * width * hidden_width,
    )
    body_after = permuted(body, ("pipe",), lambda p: ((p[0] - 1) % sections,))
    replies = call(
        functools.partial(reply_kernel, capacity),
        message_shapes(experts, size, half + LANES),
        (body_after, tail_own),
        0,
        4 * rows * half,
    )
    returned = exchanged(replies, "expert")
    grad_up, grad_down = call(
        functools.partial(weight_kernel, capacity, len(joined)),
        [
            jax.ShapeDtypeStruct((1, 1, part, hidden_width), BF16),
            jax.ShapeDtypeStruct((1, 1, hidden_width, part), BF16),
        ],
        tuple(joined),
        4 * replicas * rows * part * hidden_width,
        4 * part * hidden_width,
        near_out=False,
    )
    grad_prev, grad_gate = call(
        functools.partial(combine_kernel, capacity, sections, len(returned)),
        [
            jax.ShapeDtypeStruct((1, tokens, width), BF16),
            jax.ShapeDtypeStruct((1, 1, experts, capacity), BF16),
        ],
        tuple(returned),
        2 * rows * tokens * width,
        2 * tokens * width,
        near_out=False,
    )
    return grad_prev, grad_gate, grad_up, grad_down


def solution(mesh):
    by_token = ("dp", "expert")
    placed = (
        P("pipe", by_token, None),
        P("pipe", by_token, None),
        P("pipe", by_token, None, None),
        P("pipe", by_token, None),
        P("pipe", by_token, None, None),
        P("pipe", "expert", None, None),
        P("pipe", "expert", None, None),
    )
    return jax.shard_map(
        per_device,
        mesh=mesh,
        in_specs=placed,
        out_specs=(
            P("pipe", by_token, None),
            P("pipe", by_token, None, None),
            P("pipe", "expert", "dp", None),
            P("pipe", "expert", None, "dp"),
        ),
        check_vma=False,
    )
```

```python
import functools
import itertools

import jax
import jax.numpy as jnp
from jax import lax
from jax.experimental import pallas as pl
from jax.experimental.pallas import tpu as pltpu
from jax.sharding import PartitionSpec as P


BF16 = jnp.bfloat16
F32 = jnp.float32
LANES = 128
KERNEL_VMEM = 24 << 20
PIECES = 2


def row_marks(rows, width, capacity):
    row = lax.broadcasted_iota(jnp.int32, (rows, width), 0)
    inside = row & (2 * capacity - 1)
    group = lax.shift_right_logical(row, (2 * capacity).bit_length() - 1)
    return group, inside & (capacity - 1), inside < capacity


def stacked_rows(blocks, start, stop):
    return jnp.concatenate([block[:, start:stop].astype(F32) for block in blocks], axis=0)


def blocks_of(refs):
    if len(refs) == 1 and len(refs[0].shape) == 3:
        return [refs[0].at[k] for k in range(refs[0].shape[0])]
    return list(refs)


def in_pairs(experts, replicas):
    return experts == 4 and replicas == 4


def partner_of(group, low_first):
    side = (lax.axis_index("dp") & 1) ^ lax.shift_right_logical(group, 1)
    high = group & 1 if low_first else 1 - (group & 1)
    return 2 * high + side


def pack_kernel(acts_far, grads_far, ids_far, counts_far, probs_far, *refs):
    outs, acts, grads, ids, counts, probs, sems = refs[:-6], *refs[-6:]
    tokens, width = acts.shape[1:]
    spans = [pl.ds(k * width // PIECES, width // PIECES) for k in range(PIECES)]
    pairs = [(ids_far, ids), (counts_far, counts), (probs_far, probs)]
    for span in spans:
        pairs.append((acts_far.at[:, :, span], acts.at[:, :, span]))
        pairs.append((grads_far.at[:, :, span], grads.at[:, :, span]))
    copies = [pltpu.make_async_copy(a, b, sems.at[k]) for k, (a, b) in enumerate(pairs)]
    for copy in copies:
        copy.start()
    for copy in copies[:3]:
        copy.wait()
    experts, capacity = ids.shape[2:]
    rows = 2 * experts * capacity
    paired = in_pairs(experts, lax.axis_size("dp"))

    def dest_of(group):
        return partner_of(group, True) ^ lax.axis_index("expert") if paired else group

    group, slot, _ = row_marks(rows, capacity, capacity)
    dest = dest_of(group)
    id_rows = ids[0, 0].astype(F32)
    prob_rows = probs[0, 0].astype(F32)
    id_grid = jnp.zeros((rows, capacity), F32)
    prob_grid = jnp.zeros((rows, capacity), F32)
    for e in range(experts):
        here = dest == e
        id_grid = jnp.where(here, id_rows[e : e + 1], id_grid)
        prob_grid = jnp.where(here, prob_rows[e : e + 1], prob_grid)
    at_slot = lax.broadcasted_iota(jnp.int32, (rows, capacity), 1) == slot
    id_col = jnp.sum(jnp.where(at_slot, id_grid, 0.0), axis=1, keepdims=True)
    prob_col = jnp.sum(jnp.where(at_slot, prob_grid, 0.0), axis=1, keepdims=True)
    dest_wide = dest_of(row_marks(rows, experts, capacity)[0])
    at_dest = lax.broadcasted_iota(jnp.int32, (rows, experts), 1) == dest_wide
    count_row = counts[0].astype(F32)
    count_col = jnp.sum(jnp.where(at_dest, count_row, 0.0), axis=1, keepdims=True)
    live = slot[:, :1].astype(F32) < count_col
    prob_col = jnp.where(live, prob_col, 0.0)
    _, _, first_wide = row_marks(rows, tokens, capacity)
    lane = lax.broadcasted_iota(jnp.int32, (rows, tokens), 1).astype(F32)
    hit = jnp.where(lane == id_col, 1.0, 0.0)
    hit_live = jnp.where(live, hit, 0.0)
    pick_act = jnp.where(first_wide, hit, 0.0).astype(BF16)
    pick_grad = jnp.where(first_wide, 0.0, hit_live).astype(BF16)
    tail_lane = lax.broadcasted_iota(jnp.int32, (rows, LANES), 1)
    tail = jnp.where(tail_lane == 0, prob_col, jnp.where(tail_lane == 1, id_col, 0.0))
    blocks = blocks_of(outs)
    size = rows // len(blocks)
    for k, out in enumerate(blocks):
        out[:, width:] = tail[k * size : (k + 1) * size].astype(BF16)
    for piece, span in enumerate(spans):
        copies[3 + 2 * piece].wait()
        picked = jnp.dot(pick_act, acts[0, :, span], preferred_element_type=F32)
        copies[4 + 2 * piece].wait()
        picked = picked + jnp.dot(pick_grad, grads[0, :, span], preferred_element_type=F32)
        for k, out in enumerate(blocks):
            out[:, span] = picked[k * size : (k + 1) * size].astype(BF16)


def halves(ref):
    value = ref[...].astype(F32)
    size = ref.shape[0] // 2
    return value[:size], value[size:]


def join_kernel(kept, came, high, low):
    (kept_low, kept_high), (came_low, came_high) = halves(kept), halves(came)
    high[...] = jnp.concatenate([kept_high, came_high], axis=0).astype(BF16)
    low[...] = jnp.concatenate([kept_low, came_low], axis=0).astype(BF16)


def other_kernel(high, low, out):
    out[...] = jnp.concatenate([halves(high)[1], halves(low)[1]], axis=0).astype(BF16)


def load_kernel(up_far, down_far, _, up, down, sems):
    copies = [
        pltpu.make_async_copy(up_far, up, sems.at[0]),
        pltpu.make_async_copy(down_far, down, sems.at[1]),
    ]
    for copy in copies:
        copy.start()
    for copy in copies:
        copy.wait()


def expert_kernel(capacity, replicas, n_blocks, *refs):
    blocks = blocks_of(refs[:n_blocks])
    up, down = refs[n_blocks : n_blocks + 2]
    outs = blocks_of(refs[n_blocks + 2 : -2])
    tail_out, scaled = refs[-2:]
    width, hidden_width = up.shape[2:]
    rows = sum(block.shape[0] for block in blocks)
    part = width // replicas
    packed = stacked_rows(blocks, 0, width)
    tail = stacked_rows(blocks, width, width + LANES)
    prob = tail[:, 0:1]
    packed_bf16 = packed.astype(BF16)
    pre_act = jnp.dot(packed_bf16, up[0, 0], preferred_element_type=F32)
    grad_proj = lax.dot_general(
        packed_bf16, down[0, 0], (((1,), (1,)), ((), ())), preferred_element_type=F32
    )
    grad_proj = pltpu.roll(grad_proj, rows - capacity, 0)
    _, _, first_wide = row_marks(rows, width, capacity)
    scaled[...] = jnp.where(first_wide, packed, prob * packed).astype(BF16)
    logistic = jax.nn.sigmoid(pre_act)
    hidden = (pre_act * logistic).astype(BF16).astype(F32)
    slope = logistic * (1.0 + pre_act * (1.0 - logistic))
    act_grad = prob * grad_proj * slope
    gate = jnp.sum(hidden * grad_proj, axis=1, keepdims=True)
    lane = lax.broadcasted_iota(jnp.int32, (rows, LANES), 1)
    tail_out[...] = jnp.where(lane == 0, gate, tail).astype(BF16)
    _, _, first = row_marks(rows, hidden_width, capacity)
    both = jnp.where(first, act_grad, pltpu.roll(hidden, capacity, 0)).astype(BF16)
    place = lax.axis_index("dp") if replicas == 4 else 0
    for k, out in enumerate(outs):
        wide = out.shape[1] - hidden_width
        column = pl.multiple_of((place ^ k) // (wide // part) * wide, LANES)
        out[:, :hidden_width] = both
        out[:, hidden_width:] = scaled[:, pl.ds(column, wide)]


def back_kernel(capacity, own, up, body):
    width, hidden_width = up.shape[2:]
    half = width // 2
    row_grad = lax.dot_general(
        own[:, :hidden_width], up[0, 0], (((1,), (1,)), ((), ())), preferred_element_type=F32
    )
    _, _, first = row_marks(own.shape[0], half, capacity)
    upper = pltpu.roll(row_grad[:, half:], capacity, 0)
    body[...] = jnp.where(first, row_grad[:, :half], upper).astype(BF16)


def reply_kernel(body, tail_own, tail_other, *outs):
    rows, half = body.shape
    lane = lax.broadcasted_iota(jnp.int32, (rows, LANES), 1)
    tail = jnp.where(lane == 0, tail_other[...].astype(F32), tail_own[...].astype(F32))
    blocks = blocks_of(outs)
    size = rows // len(blocks)
    for k, out in enumerate(blocks):
        out[:, :half] = body[k * size : (k + 1) * size]
        out[:, half:] = tail[k * size : (k + 1) * size].astype(BF16)


def weight_kernel(capacity, n_blocks, *refs):
    blocks = blocks_of(refs[:n_blocks])
    grad_up, grad_down = refs[n_blocks:]
    hidden_width = grad_up.shape[3]
    part = grad_up.shape[2]
    both = jnp.concatenate([block[:, :hidden_width] for block in blocks], axis=0)
    columns = []
    for block in blocks:
        if block.shape[1] > hidden_width + part:
            begin = hidden_width + (lax.axis_index("dp") & 1) * part
            columns.append(block[:, pl.ds(pl.multiple_of(begin, LANES), part)])
        else:
            columns.append(block[:, hidden_width:])
    sides = jnp.concatenate(columns, axis=0)
    _, _, first = row_marks(both.shape[0], both.shape[1], capacity)
    act_grad = jnp.where(first, both, jnp.zeros_like(both))
    grad_up[0, 0] = lax.dot_general(
        sides, act_grad, (((0,), (0,)), ((), ())), preferred_element_type=F32
    ).astype(BF16)
    _, _, first = row_marks(sides.shape[0], sides.shape[1], capacity)
    scaled = jnp.where(first, jnp.zeros_like(sides), sides)
    grad_down[0, 0] = lax.dot_general(
        both, scaled, (((0,), (0,)), ((), ())), preferred_element_type=F32
    ).astype(BF16)


def combine_kernel(capacity, sections, n_blocks, *refs):
    blocks = blocks_of(refs[:n_blocks])
    up_near, down_near, prev_far, gate_far, up_far, down_far, prev, gate, sems = refs[n_blocks:]
    tokens, width = prev.shape[1:]
    experts = gate.shape[2]
    paired = in_pairs(experts, lax.axis_size("dp"))
    half = width // 2
    rows = 2 * capacity * experts
    spans = [pl.ds(k * half, half) for k in range(2)]
    pairs = [(prev.at[:, :, span], prev_far.at[:, :, span]) for span in spans]
    pairs += [(gate, gate_far), (up_near, up_far), (down_near, down_far)]
    copies = [pltpu.make_async_copy(a, b, sems.at[k]) for k, (a, b) in enumerate(pairs)]
    copies[3].start()
    copies[4].start()
    if paired:
        high, low, came = blocks
        joined = jnp.concatenate([halves(high)[0], halves(low)[0], *halves(came)], axis=0)
    else:
        joined = stacked_rows(blocks, 0, half + LANES)
    body, tail = joined[:, :half].astype(BF16), joined[:, half:]
    _, _, first = row_marks(rows, tokens, capacity)
    lane = lax.broadcasted_iota(jnp.int32, (rows, tokens), 1).astype(F32)
    kept = jnp.where(lax.axis_index("pipe") == sections - 1, 0.0, 1.0)
    hit = jnp.where(lane == tail[:, 1:2], kept, 0.0)
    for part, mark in enumerate((first, jnp.logical_not(first))):
        one_hot = jnp.where(mark, hit, 0.0).astype(BF16)
        prev[0, :, spans[part]] = lax.dot_general(
            one_hot, body, (((0,), (0,)), ((), ())), preferred_element_type=F32
        ).astype(BF16)
        copies[part].start()
    _, slot, first = row_marks(rows, capacity, capacity)
    at_slot = lax.broadcasted_iota(jnp.int32, (rows, capacity), 1) == slot
    gates = jnp.where(jnp.logical_and(at_slot, first), tail[:, 0:1], 0.0).astype(BF16)
    column = lax.broadcasted_iota(jnp.int32, (experts, rows), 1)
    source = lax.shift_right_logical(column, (2 * capacity).bit_length() - 1)
    if paired:
        source = partner_of(source, False) ^ lax.axis_index("expert")
    wanted = source == lax.broadcasted_iota(jnp.int32, (experts, rows), 0)
    gate[0, 0] = jnp.dot(
        jnp.where(wanted, 1.0, 0.0).astype(BF16), gates, preferred_element_type=F32
    ).astype(BF16)
    copies[2].start()
    for copy in copies:
        copy.wait()


def call(kernel, out_shape, args, flops, n_bytes, scratch=(), far=(), far_out=False):
    near_spec = pl.BlockSpec(memory_space=pltpu.VMEM)
    far_spec = pl.BlockSpec(memory_space=pl.ANY)
    args = [
        pltpu.with_memory_space_constraint(a, pltpu.HBM if k in far else pltpu.VMEM)
        for k, a in enumerate(args)
    ]
    if not far_out:
        out_shape = [pltpu.VMEM(s.shape, s.dtype) for s in out_shape]
    return pl.pallas_call(
        kernel,
        out_shape=out_shape,
        in_specs=[far_spec if k in far else near_spec for k in range(len(args))],
        out_specs=[far_spec if far_out else near_spec] * len(out_shape),
        scratch_shapes=list(scratch),
        compiler_params=pltpu.CompilerParams(vmem_limit_bytes=KERNEL_VMEM),
        cost_estimate=pl.CostEstimate(flops=flops, bytes_accessed=n_bytes, transcendentals=0),
    )(*args)


def permuted(block, axes, route):
    sizes = [lax.axis_size(axis) for axis in axes]

    def flat(place):
        return functools.reduce(lambda total, pair: total * pair[1] + pair[0], zip(place, sizes), 0)

    places = list(itertools.product(*[range(size) for size in sizes]))
    pairs = [(flat(place), flat(route(place))) for place in places]
    return lax.ppermute(block, axes if len(axes) > 1 else axes[0], pairs)


def message_shapes(paired, count, rows, width):
    if paired:
        return [jax.ShapeDtypeStruct((count * rows // 2, width), BF16)] * 2
    return [jax.ShapeDtypeStruct((count, rows, width), BF16)]


def traded(block, axis):
    return lax.all_to_all(block, axis, split_axis=0, concat_axis=0, tiled=True)


def swapped(block):
    return permuted(block, ("dp",), lambda p: (p[0] ^ 1,))


def share_shapes(replicas, rows, hidden_width, part):
    if replicas != 4:
        return message_shapes(False, replicas, rows, hidden_width + part)
    widths = (hidden_width + part, hidden_width + part, hidden_width + 2 * part)
    return [jax.ShapeDtypeStruct((rows, width), BF16) for width in widths]


def shared(blocks, replicas):
    if replicas != 4:
        return [traded(blocks[0], "dp")]
    own, near, far = blocks
    crossed = permuted(far, ("dp",), lambda p: (p[0] ^ 2,))
    beside = swapped(near)
    passed = swapped(crossed)
    return [own, beside, crossed, passed]


def per_device(activations, out_grad, slot_token, slot_count, gate_prob, w_up, w_down):
    tokens, width = activations.shape[1:]
    experts, capacity = slot_token.shape[2:]
    hidden_width = w_up.shape[3]
    replicas = lax.axis_size("dp")
    sections = lax.axis_size("pipe")
    size = 2 * capacity
    rows = size * experts
    part = width // replicas
    half = width // 2
    paired = in_pairs(experts, replicas)
    sources = (activations, out_grad, slot_token, slot_count, gate_prob)
    packed = call(
        pack_kernel,
        message_shapes(paired, experts, size, width + LANES),
        sources,
        4 * rows * tokens * width,
        4 * tokens * width,
        [pltpu.VMEM(a.shape, a.dtype) for a in sources] + [pltpu.SemaphoreType.DMA((3 + 2 * PIECES,))],
        far=range(5),
    )
    near_up, near_down = call(
        load_kernel,
        [jax.ShapeDtypeStruct(w.shape, w.dtype) for w in (w_up, w_down)],
        (w_up, w_down, packed[0]),
        0,
        4 * width * hidden_width,
        [pltpu.SemaphoreType.DMA((2,))],
        far=range(2),
    )
    if paired:
        kept, sent = packed
        high, low = call(
            join_kernel,
            message_shapes(paired, experts, size, width + LANES),
            (kept, swapped(sent)),
            0,
            4 * rows * width,
        )
        held = [
            permuted(high, ("dp", "expert"), lambda p: (p[0], p[1] ^ 2 ^ (p[0] & 1))),
            permuted(low, ("dp", "expert"), lambda p: (p[0], p[1] ^ (p[0] & 1))),
        ]
    else:
        held = [traded(packed[0], "expert")]
    made = call(
        functools.partial(expert_kernel, capacity, replicas, len(held)),
        share_shapes(replicas, rows, hidden_width, part)
        + [jax.ShapeDtypeStruct((rows, LANES), BF16)],
        (*held, near_up, near_down),
        4 * rows * width * hidden_width,
        4 * width * hidden_width,
        [pltpu.VMEM((rows, width), BF16)],
    )
    shares, tail_own = made[:-1], made[-1]
    joined = shared(shares, replicas)
    own = shares[0] if len(shares) > 1 else shares[0][0]
    tail_other = permuted(tail_own, ("pipe",), lambda p: ((p[0] + 1) % sections,))
    (body,) = call(
        functools.partial(back_kernel, capacity),
        [jax.ShapeDtypeStruct((rows, half), BF16)],
        (own, near_up),
        2 * rows * width * hidden_width,
        2 * width * hidden_width,
    )
    replies = call(
        reply_kernel,
        message_shapes(paired, experts, size, half + LANES),
        (body, tail_own, tail_other),
        0,
        4 * rows * half,
    )
    if paired:
        every = ("dp", "pipe", "expert")

        def before(p, step):
            return (p[0], (p[1] - 1) % sections, p[2] ^ step ^ (p[0] & 1))

        high = permuted(replies[0], every, lambda p: before(p, 2))
        low = permuted(replies[1], every, lambda p: before(p, 0))
        (other,) = call(
            other_kernel,
            [jax.ShapeDtypeStruct((rows // 2, half + LANES), BF16)],
            (high, low),
            0,
            4 * rows * half,
        )
        returned = [high, low, swapped(other)]
    else:
        moved = permuted(replies[0], ("pipe",), lambda p: ((p[0] - 1) % sections,))
        returned = [traded(moved, "expert")]
    weight_grads = [
        jax.ShapeDtypeStruct((1, 1, part, hidden_width), BF16),
        jax.ShapeDtypeStruct((1, 1, hidden_width, part), BF16),
    ]
    near_grads = call(
        functools.partial(weight_kernel, capacity, len(joined)),
        weight_grads,
        tuple(joined),
        4 * replicas * rows * part * hidden_width,
        4 * part * hidden_width,
    )
    token_grads = [
        jax.ShapeDtypeStruct((1, tokens, width), BF16),
        jax.ShapeDtypeStruct((1, 1, experts, capacity), BF16),
    ]
    grad_prev, grad_gate, grad_up, grad_down = call(
        functools.partial(combine_kernel, capacity, sections, len(returned)),
        token_grads + weight_grads,
        (*returned, *near_grads),
        2 * rows * tokens * width,
        2 * tokens * width,
        [pltpu.VMEM(s.shape, s.dtype) for s in token_grads] + [pltpu.SemaphoreType.DMA((5,))],
        far_out=True,
    )
    return grad_prev, grad_gate, grad_up, grad_down


def solution(mesh):
    by_token = ("dp", "expert")
    placed = (
        P("pipe", by_token, None),
        P("pipe", by_token, None),
        P("pipe", by_token, None, None),
        P("pipe", by_token, None),
        P("pipe", by_token, None, None),
        P("pipe", "expert", None, None),
        P("pipe", "expert", None, None),
    )
    return jax.shard_map(
        per_device,
        mesh=mesh,
        in_specs=placed,
        out_specs=(
            P("pipe", by_token, None),
            P("pipe", by_token, None, None),
            P("pipe", "expert", "dp", None),
            P("pipe", "expert", None, "dp"),
        ),
        check_vma=False,
    )
```

```python
import functools
import itertools

import jax
import jax.numpy as jnp
from jax import lax
from jax.experimental import pallas as pl
from jax.experimental.pallas import tpu as pltpu
from jax.sharding import PartitionSpec as P


BF16 = jnp.bfloat16
F32 = jnp.float32
LANES = 128
KERNEL_VMEM = 24 << 20
PIECES = 1


def row_marks(rows, width, capacity):
    row = lax.broadcasted_iota(jnp.int32, (rows, width), 0)
    return lax.shift_right_logical(row, capacity.bit_length() - 1), row & (capacity - 1)


def stacked(refs, columns=slice(None)):
    return jnp.concatenate([ref[:, columns].astype(F32) for ref in refs], axis=0)


def upper_rows(value):
    row = lax.broadcasted_iota(jnp.int32, value.shape, 0)
    return row < value.shape[0] // 2


def turned(value):
    return pltpu.roll(value, value.shape[0] // 2, 0)


def in_pairs(experts, replicas):
    return experts == 4 and replicas == 4


FIRST_SLOT = (2, 1)
SECOND_SLOT = (0, 3)


def partner_of(group, second_first):
    side = (lax.axis_index("dp") & 1) ^ lax.shift_right_logical(group, 1)
    second = 1 - (group & 1) if second_first else group & 1
    in_first = FIRST_SLOT[0] + side * (FIRST_SLOT[1] - FIRST_SLOT[0])
    in_second = SECOND_SLOT[0] + side * (SECOND_SLOT[1] - SECOND_SLOT[0])
    return in_first + second * (in_second - in_first)


def pack_kernel(acts_far, grads_far, ids_far, counts_far, probs_far, *refs):
    outs, acts, grads, ids, counts, probs, sems = refs[:-6], *refs[-6:]
    tokens, width = acts.shape[1:]
    spans = [pl.ds(k * width // PIECES, width // PIECES) for k in range(PIECES)]
    pairs = [(ids_far, ids), (counts_far, counts), (probs_far, probs)]
    for span in spans:
        pairs.append((acts_far.at[:, :, span], acts.at[:, :, span]))
        pairs.append((grads_far.at[:, :, span], grads.at[:, :, span]))
    copies = [pltpu.make_async_copy(a, b, sems.at[k]) for k, (a, b) in enumerate(pairs)]
    for copy in copies:
        copy.start()
    for copy in copies[:3]:
        copy.wait()
    experts, capacity = ids.shape[2:]
    rows = experts * capacity
    paired = in_pairs(experts, lax.axis_size("dp"))

    def dest_of(group):
        return partner_of(group, True) ^ lax.axis_index("expert") if paired else group

    group, slot = row_marks(rows, capacity, capacity)
    dest = dest_of(group)
    id_rows = ids[0, 0].astype(F32)
    prob_rows = probs[0, 0].astype(F32)
    id_grid = jnp.zeros((rows, capacity), F32)
    prob_grid = jnp.zeros((rows, capacity), F32)
    for e in range(experts):
        here = dest == e
        id_grid = jnp.where(here, id_rows[e : e + 1], id_grid)
        prob_grid = jnp.where(here, prob_rows[e : e + 1], prob_grid)
    at_slot = lax.broadcasted_iota(jnp.int32, (rows, capacity), 1) == slot
    id_col = jnp.sum(jnp.where(at_slot, id_grid, 0.0), axis=1, keepdims=True)
    prob_col = jnp.sum(jnp.where(at_slot, prob_grid, 0.0), axis=1, keepdims=True)
    dest_wide = dest_of(row_marks(rows, experts, capacity)[0])
    at_dest = lax.broadcasted_iota(jnp.int32, (rows, experts), 1) == dest_wide
    count_row = counts[0].astype(F32)
    count_col = jnp.sum(jnp.where(at_dest, count_row, 0.0), axis=1, keepdims=True)
    live = slot[:, :1].astype(F32) < count_col
    prob_col = jnp.where(live, prob_col, 0.0)
    lane = lax.broadcasted_iota(jnp.int32, (rows, tokens), 1).astype(F32)
    hit = jnp.where(lane == id_col, 1.0, 0.0)
    pick_act = hit.astype(BF16)
    pick_grad = jnp.where(live, hit, 0.0).astype(BF16)
    tail_lane = lax.broadcasted_iota(jnp.int32, (rows, LANES), 1)
    tail = jnp.where(tail_lane == 0, prob_col, jnp.where(tail_lane == 1, id_col, 0.0))
    size = rows // len(outs)

    def put(value, columns):
        for k, out in enumerate(outs):
            out[:, columns] = value[k * size : (k + 1) * size].astype(BF16)

    put(tail, pl.ds(2 * width, LANES))
    for piece in range(PIECES):
        step = width // PIECES
        copies[3 + 2 * piece].wait()
        picked = jnp.dot(pick_act, acts[0, :, spans[piece]], preferred_element_type=F32)
        put(picked, pl.ds(piece * step, step))
        copies[4 + 2 * piece].wait()
        picked = jnp.dot(pick_grad, grads[0, :, spans[piece]], preferred_element_type=F32)
        put(picked, pl.ds(width + piece * step, step))


def join_kernel(kept, came, first, second):
    mine, other = kept[...].astype(F32), came[...].astype(F32)
    upper = upper_rows(mine)
    first[...] = jnp.where(upper, turned(mine), other).astype(BF16)
    second[...] = jnp.where(upper, mine, turned(other)).astype(BF16)


def other_kernel(first, second, out):
    value = first[...].astype(F32)
    out[...] = jnp.where(upper_rows(value), turned(value), second[...].astype(F32)).astype(BF16)


def expert_kernel(replicas, n_blocks, *refs):
    blocks = refs[:n_blocks]
    up, down = refs[n_blocks : n_blocks + 2]
    outs = refs[n_blocks + 2 : -2]
    tail_out, scaled = refs[-2:]
    hidden_width, width = down.shape[2:]
    rows = sum(block.shape[0] for block in blocks)
    part = width // replicas
    act_rows = stacked(blocks, slice(0, width)).astype(BF16)
    pre_act = jnp.dot(act_rows, up[0, 0], preferred_element_type=F32)
    grad_rows = stacked(blocks, slice(width, 2 * width))
    tail = stacked(blocks, slice(2 * width, 2 * width + LANES))
    prob = tail[:, 0:1]
    grad_proj = lax.dot_general(
        grad_rows.astype(BF16), down[0, 0], (((1,), (1,)), ((), ())), preferred_element_type=F32
    )
    scaled[:rows] = act_rows
    scaled[rows:] = (prob * grad_rows).astype(BF16)
    logistic = jax.nn.sigmoid(pre_act)
    hidden = (pre_act * logistic).astype(BF16).astype(F32)
    slope = logistic * (1.0 + pre_act * (1.0 - logistic))
    act_grad = prob * grad_proj * slope
    gate = jnp.sum(hidden * grad_proj, axis=1, keepdims=True)
    lane = lax.broadcasted_iota(jnp.int32, (rows, LANES), 1)
    tail_out[...] = jnp.where(lane == 0, gate, tail).astype(BF16)
    both = jnp.concatenate([act_grad, hidden], axis=0).astype(BF16)
    place = lax.axis_index("dp") if replicas == 4 else 0
    for k, out in enumerate(outs if len(outs) > 1 else [outs[0].at[k] for k in range(replicas)]):
        wide = out.shape[1] - hidden_width
        column = pl.multiple_of((place ^ k) // (wide // part) * wide, LANES)
        out[:, :hidden_width] = both
        out[:, hidden_width:] = scaled[:, pl.ds(column, wide)]


def back_kernel(own, up, body):
    rows, hidden_width = body.shape[0], up.shape[3]
    body[...] = lax.dot_general(
        own[:rows, :hidden_width], up[0, 0], (((1,), (1,)), ((), ())), preferred_element_type=F32
    ).astype(BF16)


def reply_kernel(body, tail_own, tail_other, *outs):
    rows, width = body.shape
    lane = lax.broadcasted_iota(jnp.int32, (rows, LANES), 1)
    tail = jnp.where(lane == 0, tail_other[...].astype(F32), tail_own[...].astype(F32))
    values = body[...].astype(F32)
    size = rows // len(outs)
    for k, out in enumerate(outs):
        out[:, :width] = values[k * size : (k + 1) * size].astype(BF16)
        out[:, width:] = tail[k * size : (k + 1) * size].astype(BF16)


def weight_kernel(rows, n_blocks, *refs):
    blocks = refs[:n_blocks]
    if n_blocks == 1:
        blocks = [blocks[0].at[k] for k in range(blocks[0].shape[0])]
    grad_up, grad_down = refs[n_blocks:]

    def first_of(value):
        row = lax.broadcasted_iota(jnp.int32, value.shape, 0)
        return (row & (2 * rows - 1)) < rows

    hidden_width = grad_up.shape[3]
    part = grad_up.shape[2]
    both = jnp.concatenate([block[:, :hidden_width] for block in blocks], axis=0)
    columns = []
    for block in blocks:
        if block.shape[1] > hidden_width + part:
            begin = hidden_width + (lax.axis_index("dp") & 1) * part
            columns.append(block[:, pl.ds(pl.multiple_of(begin, LANES), part)])
        else:
            columns.append(block[:, hidden_width:])
    sides = jnp.concatenate(columns, axis=0)
    act_grad = jnp.where(first_of(both), both, jnp.zeros_like(both))
    grad_up[0, 0] = lax.dot_general(
        sides, act_grad, (((0,), (0,)), ((), ())), preferred_element_type=F32
    ).astype(BF16)
    scaled = jnp.where(first_of(sides), jnp.zeros_like(sides), sides)
    grad_down[0, 0] = lax.dot_general(
        both, scaled, (((0,), (0,)), ((), ())), preferred_element_type=F32
    ).astype(BF16)


def combine_kernel(capacity, sections, n_blocks, *refs):
    blocks = refs[:n_blocks]
    up_near, down_near, prev_far, gate_far, up_far, down_far, prev, gate, sems = refs[n_blocks:]
    tokens, width = prev.shape[1:]
    experts = gate.shape[2]
    paired = in_pairs(experts, lax.axis_size("dp"))
    half = width // 2
    rows = capacity * experts
    spans = [pl.ds(k * half, half) for k in range(2)]
    pairs = [(prev.at[:, :, span], prev_far.at[:, :, span]) for span in spans]
    pairs += [(gate, gate_far), (up_near, up_far), (down_near, down_far)]
    copies = [pltpu.make_async_copy(a, b, sems.at[k]) for k, (a, b) in enumerate(pairs)]
    copies[3].start()
    copies[4].start()
    if paired:
        first, second, came = [block[...].astype(F32) for block in blocks]
        mine = jnp.where(upper_rows(first), first, turned(second))
        joined = jnp.concatenate([mine, came], axis=0)
    else:
        joined = stacked(blocks)
    body, tail = joined[:, :width].astype(BF16), joined[:, width:]
    lane = lax.broadcasted_iota(jnp.int32, (rows, tokens), 1).astype(F32)
    kept = jnp.where(lax.axis_index("pipe") == sections - 1, 0.0, 1.0)
    one_hot = jnp.where(lane == tail[:, 1:2], kept, 0.0).astype(BF16)
    for part, span in enumerate(spans):
        prev[0, :, span] = lax.dot_general(
            one_hot,
            body[:, part * half : (part + 1) * half],
            (((0,), (0,)), ((), ())),
            preferred_element_type=F32,
        ).astype(BF16)
        copies[part].start()
    _, slot = row_marks(rows, capacity, capacity)
    at_slot = lax.broadcasted_iota(jnp.int32, (rows, capacity), 1) == slot
    gates = jnp.where(at_slot, tail[:, 0:1], 0.0).astype(BF16)
    column = lax.broadcasted_iota(jnp.int32, (experts, rows), 1)
    source = lax.shift_right_logical(column, capacity.bit_length() - 1)
    if paired:
        source = partner_of(source, False) ^ lax.axis_index("expert")
    wanted = source == lax.broadcasted_iota(jnp.int32, (experts, rows), 0)
    gate[0, 0] = jnp.dot(
        jnp.where(wanted, 1.0, 0.0).astype(BF16), gates, preferred_element_type=F32
    ).astype(BF16)
    copies[2].start()
    for copy in copies:
        copy.wait()


def call(kernel, out_shape, args, flops, n_bytes, scratch=(), far=(), far_out=False):
    near_spec = pl.BlockSpec(memory_space=pltpu.VMEM)
    far_spec = pl.BlockSpec(memory_space=pl.ANY)
    args = [
        pltpu.with_memory_space_constraint(a, pltpu.HBM if k in far else pltpu.VMEM)
        for k, a in enumerate(args)
    ]
    if not far_out:
        out_shape = [pltpu.VMEM(s.shape, s.dtype) for s in out_shape]
    return pl.pallas_call(
        kernel,
        out_shape=out_shape,
        in_specs=[far_spec if k in far else near_spec for k in range(len(args))],
        out_specs=[far_spec if far_out else near_spec] * len(out_shape),
        scratch_shapes=list(scratch),
        compiler_params=pltpu.CompilerParams(vmem_limit_bytes=KERNEL_VMEM),
        cost_estimate=pl.CostEstimate(flops=flops, bytes_accessed=n_bytes, transcendentals=0),
    )(*args)


def permuted(block, axes, route):
    sizes = [lax.axis_size(axis) for axis in axes]

    def flat(place):
        return functools.reduce(lambda total, pair: total * pair[1] + pair[0], zip(place, sizes), 0)

    places = list(itertools.product(*[range(size) for size in sizes]))
    pairs = [(flat(place), flat(route(place))) for place in places]
    return lax.ppermute(block, axes if len(axes) > 1 else axes[0], pairs)


def message_shapes(paired, rows, width, dtype=BF16):
    if paired:
        return [jax.ShapeDtypeStruct((rows // 2, width), dtype)] * 2
    return [jax.ShapeDtypeStruct((rows, width), dtype)]


def traded(block, axis):
    return lax.all_to_all(block, axis, split_axis=0, concat_axis=0, tiled=True)


def swapped(block):
    return permuted(block, ("dp",), lambda p: (p[0] ^ 1,))


def share_shapes(replicas, rows, hidden_width, part):
    if replicas != 4:
        return [jax.ShapeDtypeStruct((replicas, rows, hidden_width + part), BF16)]
    widths = (hidden_width + part, hidden_width + part, hidden_width + 2 * part)
    return [jax.ShapeDtypeStruct((rows, width), BF16) for width in widths]


def shared(blocks, replicas):
    if replicas != 4:
        return [traded(blocks[0], "dp")]
    own, near, far = blocks
    crossed = permuted(far, ("dp",), lambda p: (p[0] ^ 2,))
    beside = swapped(near)
    passed = swapped(crossed)
    return [own, beside, crossed, passed]


def per_device(activations, out_grad, slot_token, slot_count, gate_prob, w_up, w_down):
    tokens, width = activations.shape[1:]
    experts, capacity = slot_token.shape[2:]
    hidden_width = w_up.shape[3]
    replicas = lax.axis_size("dp")
    sections = lax.axis_size("pipe")
    rows = capacity * experts
    part = width // replicas
    paired = in_pairs(experts, replicas)
    sources = (activations, out_grad, slot_token, slot_count, gate_prob)
    packed = call(
        pack_kernel,
        message_shapes(paired, rows, 2 * width + LANES),
        sources,
        4 * rows * tokens * width,
        4 * tokens * width,
        [pltpu.VMEM(a.shape, a.dtype) for a in sources] + [pltpu.SemaphoreType.DMA((3 + 2 * PIECES,))],
        far=range(5),
    )
    if paired:
        kept, sent = packed
        first, second = call(
            join_kernel,
            message_shapes(paired, rows, 2 * width + LANES),
            (kept, swapped(sent)),
            20_000_000_000,
            4 * rows * width,
        )
        across = ("dp", "expert")

        def first_slot(p):
            return (p[0], p[1] ^ FIRST_SLOT[p[0] & 1])

        def second_slot(p):
            return (p[0], p[1] ^ SECOND_SLOT[p[0] & 1])

        held = [permuted(first, across, first_slot), permuted(second, across, second_slot)]
    else:
        held = [traded(packed[0], "expert")]
    made = call(
        functools.partial(expert_kernel, replicas, len(held)),
        share_shapes(replicas, 2 * rows, hidden_width, part)
        + [jax.ShapeDtypeStruct((rows, LANES), BF16)],
        (*held, w_up, w_down),
        4 * rows * width * hidden_width,
        4 * width * hidden_width,
        [pltpu.VMEM((2 * rows, width), BF16)],
    )
    shares, tail_own = made[:-1], made[-1]
    joined = shared(shares, replicas)
    own = shares[0] if len(shares) > 1 else shares[0][0]
    tail_other = permuted(tail_own, ("pipe",), lambda p: ((p[0] + 1) % sections,))
    (body,) = call(
        back_kernel,
        [jax.ShapeDtypeStruct((rows, width), BF16)],
        (own, w_up),
        2 * rows * width * hidden_width,
        2 * width * hidden_width,
    )
    replies = call(
        reply_kernel,
        message_shapes(paired, rows, width + LANES),
        (body, tail_own, tail_other),
        0,
        4 * rows * width,
    )
    if paired:
        every = ("dp", "pipe", "expert")

        def before(p, slot):
            return (p[0], (p[1] - 1) % sections, p[2] ^ slot[p[0] & 1])

        high = permuted(replies[0], every, lambda p: before(p, FIRST_SLOT))
        low = permuted(replies[1], every, lambda p: before(p, SECOND_SLOT))
        (other,) = call(
            other_kernel,
            [jax.ShapeDtypeStruct((rows // 2, width + LANES), BF16)],
            (high, low),
            0,
            4 * rows * width,
        )
        returned = [high, low, swapped(other)]
    else:
        moved = permuted(replies[0], ("pipe",), lambda p: ((p[0] - 1) % sections,))
        returned = [traded(moved, "expert")]
    weight_grads = [
        jax.ShapeDtypeStruct((1, 1, part, hidden_width), BF16),
        jax.ShapeDtypeStruct((1, 1, hidden_width, part), BF16),
    ]
    near_grads = call(
        functools.partial(weight_kernel, rows, len(joined)),
        weight_grads,
        tuple(joined),
        4 * replicas * rows * part * hidden_width,
        4 * part * hidden_width,
    )
    token_grads = [
        jax.ShapeDtypeStruct((1, tokens, width), BF16),
        jax.ShapeDtypeStruct((1, 1, experts, capacity), BF16),
    ]
    grad_prev, grad_gate, grad_up, grad_down = call(
        functools.partial(combine_kernel, capacity, sections, len(returned)),
        token_grads + weight_grads,
        (*returned, *near_grads),
        2 * rows * tokens * width,
        2 * tokens * width,
        [pltpu.VMEM(s.shape, s.dtype) for s in token_grads] + [pltpu.SemaphoreType.DMA((5,))],
        far_out=True,
    )
    return grad_prev, grad_gate, grad_up, grad_down


def solution(mesh):
    by_token = ("dp", "expert")
    placed = (
        P("pipe", by_token, None),
        P("pipe", by_token, None),
        P("pipe", by_token, None, None),
        P("pipe", by_token, None),
        P("pipe", by_token, None, None),
        P("pipe", "expert", None, None),
        P("pipe", "expert", None, None),
    )
    return jax.shard_map(
        per_device,
        mesh=mesh,
        in_specs=placed,
        out_specs=(
            P("pipe", by_token, None),
            P("pipe", by_token, None, None),
            P("pipe", "expert", "dp", None),
            P("pipe", "expert", None, "dp"),
        ),
        check_vma=False,
    )
```

```python
import functools
import itertools

import jax
import jax.numpy as jnp
from jax import lax
from jax.experimental import pallas as pl
from jax.experimental.pallas import tpu as pltpu
from jax.sharding import PartitionSpec as P


BF16 = jnp.bfloat16
F32 = jnp.float32
LANES = 128
KERNEL_VMEM = 24 << 20
PIECES = 1


def row_marks(rows, width, capacity):
    row = lax.broadcasted_iota(jnp.int32, (rows, width), 0)
    return lax.shift_right_logical(row, capacity.bit_length() - 1), row & (capacity - 1)


def stacked(refs, columns=slice(None)):
    return jnp.concatenate([ref[:, columns].astype(F32) for ref in refs], axis=0)


def upper_rows(value):
    row = lax.broadcasted_iota(jnp.int32, value.shape, 0)
    return row < value.shape[0] // 2


def turned(value):
    return pltpu.roll(value, value.shape[0] // 2, 0)


def in_pairs(experts, replicas):
    return experts == 4 and replicas == 4


FIRST_SLOT = (2, 1)
SECOND_SLOT = (0, 3)


def partner_of(group, second_first):
    side = (lax.axis_index("dp") & 1) ^ lax.shift_right_logical(group, 1)
    second = 1 - (group & 1) if second_first else group & 1
    in_first = FIRST_SLOT[0] + side * (FIRST_SLOT[1] - FIRST_SLOT[0])
    in_second = SECOND_SLOT[0] + side * (SECOND_SLOT[1] - SECOND_SLOT[0])
    return in_first + second * (in_second - in_first)


def pack_kernel(acts_far, grads_far, ids_far, counts_far, probs_far, *refs):
    outs, acts, grads, ids, counts, probs, sems = refs[:-6], *refs[-6:]
    tokens, width = acts.shape[1:]
    spans = [pl.ds(k * width // PIECES, width // PIECES) for k in range(PIECES)]
    pairs = [(ids_far, ids), (counts_far, counts), (probs_far, probs)]
    for span in spans:
        pairs.append((acts_far.at[:, :, span], acts.at[:, :, span]))
        pairs.append((grads_far.at[:, :, span], grads.at[:, :, span]))
    copies = [pltpu.make_async_copy(a, b, sems.at[k]) for k, (a, b) in enumerate(pairs)]
    for copy in copies:
        copy.start()
    for copy in copies[:3]:
        copy.wait()
    experts, capacity = ids.shape[2:]
    rows = experts * capacity
    paired = in_pairs(experts, lax.axis_size("dp"))

    def dest_of(group):
        return partner_of(group, True) ^ lax.axis_index("expert") if paired else group

    group, slot = row_marks(rows, capacity, capacity)
    dest = dest_of(group)
    id_rows = ids[0, 0].astype(F32)
    prob_rows = probs[0, 0].astype(F32)
    id_grid = jnp.zeros((rows, capacity), F32)
    prob_grid = jnp.zeros((rows, capacity), F32)
    for e in range(experts):
        here = dest == e
        id_grid = jnp.where(here, id_rows[e : e + 1], id_grid)
        prob_grid = jnp.where(here, prob_rows[e : e + 1], prob_grid)
    at_slot = lax.broadcasted_iota(jnp.int32, (rows, capacity), 1) == slot
    id_col = jnp.sum(jnp.where(at_slot, id_grid, 0.0), axis=1, keepdims=True)
    prob_col = jnp.sum(jnp.where(at_slot, prob_grid, 0.0), axis=1, keepdims=True)
    dest_wide = dest_of(row_marks(rows, experts, capacity)[0])
    at_dest = lax.broadcasted_iota(jnp.int32, (rows, experts), 1) == dest_wide
    count_row = counts[0].astype(F32)
    count_col = jnp.sum(jnp.where(at_dest, count_row, 0.0), axis=1, keepdims=True)
    live = slot[:, :1].astype(F32) < count_col
    prob_col = jnp.where(live, prob_col, 0.0)
    lane = lax.broadcasted_iota(jnp.int32, (rows, tokens), 1).astype(F32)
    hit = jnp.where(lane == id_col, 1.0, 0.0)
    pick_act = hit.astype(BF16)
    pick_grad = jnp.where(live, hit, 0.0).astype(BF16)
    tail_lane = lax.broadcasted_iota(jnp.int32, (rows, LANES), 1)
    tail = jnp.where(tail_lane == 0, prob_col, jnp.where(tail_lane == 1, id_col, 0.0))
    size = rows // len(outs)

    def put(value, columns):
        for k, out in enumerate(outs):
            out[:, columns] = value[k * size : (k + 1) * size].astype(BF16)

    put(tail, pl.ds(2 * width, LANES))
    for piece in range(PIECES):
        step = width // PIECES
        copies[3 + 2 * piece].wait()
        picked = jnp.dot(pick_act, acts[0, :, spans[piece]], preferred_element_type=F32)
        put(picked, pl.ds(piece * step, step))
        copies[4 + 2 * piece].wait()
        picked = jnp.dot(pick_grad, grads[0, :, spans[piece]], preferred_element_type=F32)
        put(picked, pl.ds(width + piece * step, step))


def join_kernel(kept, came, first, second):
    mine, other = kept[...].astype(F32), came[...].astype(F32)
    upper = upper_rows(mine)
    first[...] = jnp.where(upper, turned(mine), other).astype(BF16)
    second[...] = jnp.where(upper, mine, turned(other)).astype(BF16)


def other_kernel(first, second, out):
    value = first[...].astype(F32)
    out[...] = jnp.where(upper_rows(value), turned(value), second[...].astype(F32)).astype(BF16)


def expert_kernel(replicas, n_blocks, *refs):
    blocks = refs[:n_blocks]
    up, down = refs[n_blocks : n_blocks + 2]
    outs = refs[n_blocks + 2 : -2]
    tail_out, scaled = refs[-2:]
    hidden_width, width = down.shape[2:]
    rows = sum(block.shape[0] for block in blocks)
    part = width // replicas
    act_rows = stacked(blocks, slice(0, width)).astype(BF16)
    pre_act = jnp.dot(act_rows, up[0, 0], preferred_element_type=F32)
    grad_rows = stacked(blocks, slice(width, 2 * width))
    tail = stacked(blocks, slice(2 * width, 2 * width + LANES))
    prob = tail[:, 0:1]
    grad_proj = lax.dot_general(
        grad_rows.astype(BF16), down[0, 0], (((1,), (1,)), ((), ())), preferred_element_type=F32
    )
    scaled[:rows] = act_rows
    scaled[rows:] = (prob * grad_rows).astype(BF16)
    logistic = jax.nn.sigmoid(pre_act)
    hidden = (pre_act * logistic).astype(BF16).astype(F32)
    slope = logistic * (1.0 + pre_act * (1.0 - logistic))
    act_grad = prob * grad_proj * slope
    gate = jnp.sum(hidden * grad_proj, axis=1, keepdims=True)
    lane = lax.broadcasted_iota(jnp.int32, (rows, LANES), 1)
    tail_out[...] = jnp.where(lane == 0, gate, tail).astype(BF16)
    both = jnp.concatenate([act_grad, hidden], axis=0).astype(BF16)
    place = lax.axis_index("dp") if replicas == 4 else 0
    for k, out in enumerate(outs if len(outs) > 1 else [outs[0].at[k] for k in range(replicas)]):
        wide = out.shape[1] - hidden_width
        column = pl.multiple_of((place ^ k) // (wide // part) * wide, LANES)
        out[:, :hidden_width] = both
        out[:, hidden_width:] = scaled[:, pl.ds(column, wide)]


def back_kernel(own, up, body):
    rows, hidden_width = body.shape[0], up.shape[3]
    body[...] = lax.dot_general(
        own[:rows, :hidden_width], up[0, 0], (((1,), (1,)), ((), ())), preferred_element_type=F32
    ).astype(BF16)


def reply_kernel(body, tail_own, tail_other, *outs):
    rows, width = body.shape
    lane = lax.broadcasted_iota(jnp.int32, (rows, LANES), 1)
    tail = jnp.where(lane == 0, tail_other[...].astype(F32), tail_own[...].astype(F32))
    values = body[...].astype(F32)
    size = rows // len(outs)
    for k, out in enumerate(outs):
        out[:, :width] = values[k * size : (k + 1) * size].astype(BF16)
        out[:, width:] = tail[k * size : (k + 1) * size].astype(BF16)


def weight_kernel(rows, n_blocks, *refs):
    blocks = refs[:n_blocks]
    if n_blocks == 1:
        blocks = [blocks[0].at[k] for k in range(blocks[0].shape[0])]
    up_far, grad_down, grad_up, sem = refs[n_blocks:]
    up_out = pltpu.make_async_copy(grad_up, up_far, sem.at[0])

    def first_of(value):
        row = lax.broadcasted_iota(jnp.int32, value.shape, 0)
        return (row & (2 * rows - 1)) < rows

    hidden_width = grad_up.shape[3]
    part = grad_up.shape[2]
    both = jnp.concatenate([block[:, :hidden_width] for block in blocks], axis=0)
    columns = []
    for block in blocks:
        if block.shape[1] > hidden_width + part:
            begin = hidden_width + (lax.axis_index("dp") & 1) * part
            columns.append(block[:, pl.ds(pl.multiple_of(begin, LANES), part)])
        else:
            columns.append(block[:, hidden_width:])
    sides = jnp.concatenate(columns, axis=0)
    act_grad = jnp.where(first_of(both), both, jnp.zeros_like(both))
    grad_up[0, 0] = lax.dot_general(
        sides, act_grad, (((0,), (0,)), ((), ())), preferred_element_type=F32
    ).astype(BF16)
    up_out.start()
    scaled = jnp.where(first_of(sides), jnp.zeros_like(sides), sides)
    grad_down[0, 0] = lax.dot_general(
        both, scaled, (((0,), (0,)), ((), ())), preferred_element_type=F32
    ).astype(BF16)
    up_out.wait()


def flush_kernel(down, _, down_far, sem):
    copy = pltpu.make_async_copy(down, down_far, sem.at[0])
    copy.start()
    copy.wait()


def combine_kernel(capacity, sections, n_blocks, *refs):
    blocks = refs[:n_blocks]
    prev_far, gate_far, prev, gate, sems = refs[n_blocks:]
    tokens, width = prev.shape[1:]
    experts = gate.shape[2]
    paired = in_pairs(experts, lax.axis_size("dp"))
    half = width // 2
    rows = capacity * experts
    spans = [pl.ds(k * half, half) for k in range(2)]
    pairs = [(prev.at[:, :, span], prev_far.at[:, :, span]) for span in spans]
    pairs.append((gate, gate_far))
    copies = [pltpu.make_async_copy(a, b, sems.at[k]) for k, (a, b) in enumerate(pairs)]
    if paired:
        first, second, came = [block[...].astype(F32) for block in blocks]
        mine = jnp.where(upper_rows(first), first, turned(second))
        joined = jnp.concatenate([mine, came], axis=0)
    else:
        joined = stacked(blocks)
    body, tail = joined[:, :width].astype(BF16), joined[:, width:]
    lane = lax.broadcasted_iota(jnp.int32, (rows, tokens), 1).astype(F32)
    kept = jnp.where(lax.axis_index("pipe") == sections - 1, 0.0, 1.0)
    one_hot = jnp.where(lane == tail[:, 1:2], kept, 0.0).astype(BF16)
    for part, span in enumerate(spans):
        prev[0, :, span] = lax.dot_general(
            one_hot,
            body[:, part * half : (part + 1) * half],
            (((0,), (0,)), ((), ())),
            preferred_element_type=F32,
        ).astype(BF16)
        copies[part].start()
    _, slot = row_marks(rows, capacity, capacity)
    at_slot = lax.broadcasted_iota(jnp.int32, (rows, capacity), 1) == slot
    gates = jnp.where(at_slot, tail[:, 0:1], 0.0).astype(BF16)
    column = lax.broadcasted_iota(jnp.int32, (experts, rows), 1)
    source = lax.shift_right_logical(column, capacity.bit_length() - 1)
    if paired:
        source = partner_of(source, False) ^ lax.axis_index("expert")
    wanted = source == lax.broadcasted_iota(jnp.int32, (experts, rows), 0)
    gate[0, 0] = jnp.dot(
        jnp.where(wanted, 1.0, 0.0).astype(BF16), gates, preferred_element_type=F32
    ).astype(BF16)
    copies[2].start()
    for copy in copies:
        copy.wait()


def call(kernel, out_shape, args, flops, n_bytes, scratch=(), far=(), far_out=()):
    near_spec = pl.BlockSpec(memory_space=pltpu.VMEM)
    far_spec = pl.BlockSpec(memory_space=pl.ANY)
    args = [
        pltpu.with_memory_space_constraint(a, pltpu.HBM if k in far else pltpu.VMEM)
        for k, a in enumerate(args)
    ]
    out_shape = [
        s if k in far_out else pltpu.VMEM(s.shape, s.dtype) for k, s in enumerate(out_shape)
    ]
    return pl.pallas_call(
        kernel,
        out_shape=out_shape,
        in_specs=[far_spec if k in far else near_spec for k in range(len(args))],
        out_specs=[far_spec if k in far_out else near_spec for k in range(len(out_shape))],
        scratch_shapes=list(scratch),
        compiler_params=pltpu.CompilerParams(vmem_limit_bytes=KERNEL_VMEM),
        cost_estimate=pl.CostEstimate(flops=flops, bytes_accessed=n_bytes, transcendentals=0),
    )(*args)


def permuted(block, axes, route):
    sizes = [lax.axis_size(axis) for axis in axes]

    def flat(place):
        return functools.reduce(lambda total, pair: total * pair[1] + pair[0], zip(place, sizes), 0)

    places = list(itertools.product(*[range(size) for size in sizes]))
    pairs = [(flat(place), flat(route(place))) for place in places]
    return lax.ppermute(block, axes if len(axes) > 1 else axes[0], pairs)


def message_shapes(paired, rows, width, dtype=BF16):
    if paired:
        return [jax.ShapeDtypeStruct((rows // 2, width), dtype)] * 2
    return [jax.ShapeDtypeStruct((rows, width), dtype)]


def traded(block, axis):
    return lax.all_to_all(block, axis, split_axis=0, concat_axis=0, tiled=True)


def swapped(block):
    return permuted(block, ("dp",), lambda p: (p[0] ^ 1,))


def share_shapes(replicas, rows, hidden_width, part):
    if replicas != 4:
        return [jax.ShapeDtypeStruct((replicas, rows, hidden_width + part), BF16)]
    widths = (hidden_width + part, hidden_width + part, hidden_width + 2 * part)
    return [jax.ShapeDtypeStruct((rows, width), BF16) for width in widths]


def shared(blocks, replicas):
    if replicas != 4:
        return [traded(blocks[0], "dp")]
    own, near, far = blocks
    crossed = permuted(far, ("dp",), lambda p: (p[0] ^ 2,))
    beside = swapped(near)
    passed = swapped(crossed)
    return [own, beside, crossed, passed]


def per_device(activations, out_grad, slot_token, slot_count, gate_prob, w_up, w_down):
    tokens, width = activations.shape[1:]
    experts, capacity = slot_token.shape[2:]
    hidden_width = w_up.shape[3]
    replicas = lax.axis_size("dp")
    sections = lax.axis_size("pipe")
    rows = capacity * experts
    part = width // replicas
    paired = in_pairs(experts, replicas)
    sources = (activations, out_grad, slot_token, slot_count, gate_prob)
    packed = call(
        pack_kernel,
        message_shapes(paired, rows, 2 * width + LANES),
        sources,
        4 * rows * tokens * width,
        4 * tokens * width,
        [pltpu.VMEM(a.shape, a.dtype) for a in sources] + [pltpu.SemaphoreType.DMA((3 + 2 * PIECES,))],
        far=range(5),
    )
    if paired:
        kept, sent = packed
        first, second = call(
            join_kernel,
            message_shapes(paired, rows, 2 * width + LANES),
            (kept, swapped(sent)),
            20_000_000_000,
            4 * rows * width,
        )
        across = ("dp", "expert")

        def first_slot(p):
            return (p[0], p[1] ^ FIRST_SLOT[p[0] & 1])

        def second_slot(p):
            return (p[0], p[1] ^ SECOND_SLOT[p[0] & 1])

        held = [permuted(first, across, first_slot), permuted(second, across, second_slot)]
    else:
        held = [traded(packed[0], "expert")]
    made = call(
        functools.partial(expert_kernel, replicas, len(held)),
        share_shapes(replicas, 2 * rows, hidden_width, part)
        + [jax.ShapeDtypeStruct((rows, LANES), BF16)],
        (*held, w_up, w_down),
        4 * rows * width * hidden_width,
        4 * width * hidden_width,
        [pltpu.VMEM((2 * rows, width), BF16)],
    )
    shares, tail_own = made[:-1], made[-1]
    joined = shared(shares, replicas)
    own = shares[0] if len(shares) > 1 else shares[0][0]
    tail_other = permuted(tail_own, ("pipe",), lambda p: ((p[0] + 1) % sections,))
    (body,) = call(
        back_kernel,
        [jax.ShapeDtypeStruct((rows, width), BF16)],
        (own, w_up),
        2 * rows * width * hidden_width,
        2 * width * hidden_width,
    )
    replies = call(
        reply_kernel,
        message_shapes(paired, rows, width + LANES),
        (body, tail_own, tail_other),
        0,
        4 * rows * width,
    )
    if paired:
        every = ("dp", "pipe", "expert")

        def before(p, slot):
            return (p[0], (p[1] - 1) % sections, p[2] ^ slot[p[0] & 1])

        high = permuted(replies[0], every, lambda p: before(p, FIRST_SLOT))
        low = permuted(replies[1], every, lambda p: before(p, SECOND_SLOT))
        (other,) = call(
            other_kernel,
            [jax.ShapeDtypeStruct((rows // 2, width + LANES), BF16)],
            (high, low),
            0,
            4 * rows * width,
        )
        returned = [high, low, swapped(other)]
    else:
        moved = permuted(replies[0], ("pipe",), lambda p: ((p[0] - 1) % sections,))
        returned = [traded(moved, "expert")]
    weight_grads = [
        jax.ShapeDtypeStruct((1, 1, part, hidden_width), BF16),
        jax.ShapeDtypeStruct((1, 1, hidden_width, part), BF16),
    ]
    grad_up, near_down = call(
        functools.partial(weight_kernel, rows, len(joined)),
        weight_grads,
        tuple(joined),
        4 * replicas * rows * part * hidden_width,
        4 * part * hidden_width,
        [pltpu.VMEM(weight_grads[0].shape, BF16), pltpu.SemaphoreType.DMA((1,))],
        far_out=(0,),
    )
    (grad_down,) = call(
        flush_kernel,
        weight_grads[1:],
        (near_down, returned[0]),
        0,
        8 * part * hidden_width,
        [pltpu.SemaphoreType.DMA((1,))],
        far_out=(0,),
    )
    token_grads = [
        jax.ShapeDtypeStruct((1, tokens, width), BF16),
        jax.ShapeDtypeStruct((1, 1, experts, capacity), BF16),
    ]
    grad_prev, grad_gate = call(
        functools.partial(combine_kernel, capacity, sections, len(returned)),
        token_grads,
        tuple(returned),
        2 * rows * tokens * width,
        2 * tokens * width,
        [pltpu.VMEM(s.shape, s.dtype) for s in token_grads] + [pltpu.SemaphoreType.DMA((3,))],
        far_out=(0, 1),
    )
    return grad_prev, grad_gate, grad_up, grad_down


def solution(mesh):
    by_token = ("dp", "expert")
    placed = (
        P("pipe", by_token, None),
        P("pipe", by_token, None),
        P("pipe", by_token, None, None),
        P("pipe", by_token, None),
        P("pipe", by_token, None, None),
        P("pipe", "expert", None, None),
        P("pipe", "expert", None, None),
    )
    return jax.shard_map(
        per_device,
        mesh=mesh,
        in_specs=placed,
        out_specs=(
            P("pipe", by_token, None),
            P("pipe", by_token, None, None),
            P("pipe", "expert", "dp", None),
            P("pipe", "expert", None, "dp"),
        ),
        check_vma=False,
    )
```
